256 devices in a mesh: seq: 16 (over y_hi, z), batch: 16 (over y_lo, x, core).
Axes of the slice: x: 4, y: 4 (y_hi: 2, y_lo: 2; y = y_hi * 2 + y_lo), z: 8, core: 2. Of those that a mesh axis runs over, the one named last changes fastest.
Arguments:
- tokens: bfloat16 [16, 8192, 1536], P('batch', 'seq'), may hold values from -24 to 24
- filter_tap_weight: float32 [5, 1536], replicated, may hold values from -2.4 to 2.4
- norm_gain: float32 [1536], replicated, may hold values from 0.5 to 1.5
- query_weight: bfloat16 [1536, 512], replicated, may hold values from -4 to 4
- keyval_weight: bfloat16 [1536, 320], replicated, may hold values from -1 to 1
- head_weight: bfloat16 [768, 2, 384], replicated, may hold values from -0.21875 to 0.21875
- head_bias: float32 [2, 384], replicated, may hold values from -1 to 1
- exon_start: int32 [16, 32, 8], P('batch'), may hold values from 0 to 8191, as said below
- exon_end: int32 [16, 32, 8], P('batch'), may hold values from 0 to 8192, as said below
- gene_strand: int32 [16, 32], P('batch'), may hold values from 0 to 1
- gene_owner: int32 [16, 32, 1], P('batch'), may hold values from 0 to 15; in each aligned block of 32 rows (0 to 31, 32 to 63, ..., all dimensions but the last counted through in order) at most 4 rows name the same one
- gene_target: float32 [16, 16, 4, 384], P('batch'), may hold values from 0 to 4
Outputs:
- coverage: bfloat16 [16, 8192, 2, 384], P('batch', 'seq')
- gene_pred: float32 [16, 16, 4, 384], P('batch')
- head_grad: float32 [768, 2, 384], replicated
- bias_grad: float32 [2, 384], replicated
The draws below stay inside these ranges and needn't reach their ends.
Inputs may be any that keep to these rules, and one draw needn't show every extreme that they name: `exon_start`: exons of a gene lie inside the window in increasing order without intersection, each of 1 to 4 bins; unused exon slots have start equal to end; every gene has at least one exon. `exon_end`: as exon_start. `gene_owner`: at most 4 genes of one window have the same owner.
All inputs are finite; a program needn't handle non-finite values.
Results may differ from the reference program's by a relative error of at most 0.025.
Values may be sent and summed in bfloat16 or wider, within the bound.
No kernel may reach another device: no remote copies, remote signals or barrier semaphores. Data moves between devices by JAX's collectives and lax.ppermute only.
A program may use at most 64 MiB of HBM per device.

```python
import math
import jax
import jax.numpy as jnp
import numpy as np
from jax import lax

C = 1536
HEADS = 4
DK = 128
DV = 192
TRK = 384
FILTER_TAP_COUNT = 5
DILATION_STRIDE = 64
EXLEN = 4
EXONS = 8
ROWS = 512
GENES = 32
WINDOW_BIN_COUNT = 8192
WINDOWS = 16
CAP = 4
N_BATCH = 16


def exon_bounds(key):
    band = WINDOW_BIN_COUNT // (2 * EXONS)
    span_bins = EXONS * band
    first_key, live_key, size_key, shift_key = jax.random.split(jax.random.fold_in(key, 7), 4)
    shape_full = (WINDOWS, GENES, EXONS)
    gene_index = jnp.arange(GENES, dtype=jnp.int32)[None, :, None]
    exon_index = jnp.arange(EXONS, dtype=jnp.int32)[None, None, :]
    begins = jax.random.randint(first_key, (WINDOWS, GENES, 1), 0, WINDOW_BIN_COUNT - span_bins + 1, dtype=jnp.int32)
    begins = jnp.where(gene_index == 0, 0, jnp.where(gene_index == 1, WINDOW_BIN_COUNT - span_bins, begins)).astype(jnp.int32)
    live_count = jax.random.randint(live_key, (WINDOWS, GENES, 1), 1, EXONS + 1, dtype=jnp.int32)
    live_count = jnp.where(gene_index == 1, EXONS, live_count).astype(jnp.int32)
    sizes = jax.random.randint(size_key, shape_full, 1, EXLEN + 1, dtype=jnp.int32)
    room_left = band - sizes
    shifts = jax.random.randint(shift_key, shape_full, 0, room_left + 1, dtype=jnp.int32)
    shifts = jnp.where((gene_index == 0) & (exon_index == 0), 0, shifts)
    shifts = jnp.where((gene_index == 1) & (exon_index == EXONS - 1), room_left, shifts).astype(jnp.int32)
    starts = begins + exon_index * band + shifts
    used = exon_index < live_count
    return (jnp.where(used, starts, begins).astype(jnp.int32), jnp.where(used, starts + sizes, begins).astype(jnp.int32))


def draw_exon_start(key, part):
    return exon_bounds(key)[0]


def draw_exon_end(key, part):
    return exon_bounds(key)[1]


def attention_weights(key):
    base_key, query_key = jax.random.split(jax.random.fold_in(key, 11), 2)
    keyval = jax.random.truncated_normal(base_key, -6.0, 6.0, (C, DK + DV), jnp.float32) * C ** (-0.5)
    noise = jax.random.truncated_normal(query_key, -6.0, 6.0, (C, HEADS, DK), jnp.float32)
    query = 3.0 * C ** (-0.5) * noise
    return (jnp.clip(query.reshape(C, HEADS * DK), -4.0, 4.0), keyval)


def draw_query_weight(key, part):
    return attention_weights(key)[0].astype(jnp.bfloat16)


def draw_keyval_weight(key, part):
    return attention_weights(key)[1].astype(jnp.bfloat16)


def draw_tokens(key, part):
    base_key = jax.random.fold_in(jax.random.fold_in(key, 3), 0)
    return jax.random.truncated_normal(base_key, -6.0, 6.0, (WINDOWS, WINDOW_BIN_COUNT, C), jnp.float32).astype(jnp.bfloat16)


def touch_ends(values, own_key, low, largest):
    dims = values.shape
    index_at = [jax.random.randint(jax.random.fold_in(own_key, axis), (), 0, dims[axis]) for axis in range(len(dims))]
    values = values.at[tuple(index_at)].set(low)
    longest = dims.index(max(dims))
    index_at[longest] = (index_at[longest] + 1) % dims[longest]
    return values.at[tuple(index_at)].set(largest)


def steps_of(key, dims, cuts, least, top_value):
    gain, own = 1.0, jax.random.fold_in(key, 6)
    for dim, blocks in cuts:
        draws = jnp.exp(jax.random.uniform(jax.random.fold_in(own, dim), (blocks,), jnp.float32, least / len(cuts), top_value / len(cuts)))
        gain = gain * jnp.repeat(draws, dims[dim] // blocks).reshape([-1 if axis == dim else 1 for axis in range(len(dims))])
    return gain


def deal_out(own_key, own, number, rows, number_of, top, bound, slope):
    ranking = jax.random.permutation(own_key, number_of)
    packed, common = portions_of(number_of, rows * top, bound, slope, True), portions_of(number_of, rows * top, bound, slope, False)
    places = jnp.arange(number_of)

    def named(sizes, offset_by):
        used = int((sizes > 0).sum())
        fixed = max(1, used // 4)
        passed = fixed + (places - fixed + offset_by * (used - fixed)) % max(1, number_of - fixed)
        return jnp.zeros((number_of,), jnp.int32).at[ranking[jnp.where(places < fixed, places, passed)]].set(jnp.asarray(sizes, jnp.int32))

    sizes = jnp.where(number % 4 == 0, named(packed, number // 4), named(common, number - number // 4 - 1))
    mixed = jax.random.permutation(jax.random.fold_in(own, 3), number_of)
    donor, receiver = mixed[0:number_of // 2 * 2:2], mixed[1:number_of // 2 * 2:2]
    room = jnp.minimum(sizes[donor] - 1, bound - sizes[receiver]) // 2
    room = jnp.where((donor == ranking[0]) | (receiver == ranking[0]) | (sizes[receiver] == 0), 0, jnp.maximum(room, 0))
    passed = jax.random.randint(jax.random.fold_in(own, 4), (number_of // 2,), 0, 1 << 20) % (room + 1)
    sizes = sizes.at[donor].add(-passed).at[receiver].add(passed)
    items = jnp.searchsorted(jnp.cumsum(sizes), jnp.arange(rows * top), side="right").astype(jnp.int32)
    listing = items.reshape(top, rows).T
    listing = listing[jax.random.permutation(jax.random.fold_in(own, 1), rows)]
    offset_by = jax.random.randint(jax.random.fold_in(own, 2), (rows, 1), 0, top)
    return jnp.take_along_axis(listing, (jnp.arange(top)[None, :] + offset_by) % top, axis=1)


def portions_of(number_of, total, most, lean, full):
    portions = [(1 << 20) // math.isqrt(rank ** lean) + 1 for rank in range(1, number_of + 1)]
    largest = most if full else min(most, max(-(-total // number_of), total * portions[0] // sum(portions)))
    least = 1 if total - largest >= number_of - 1 else 0
    holding, surplus = [largest] + [least] * (number_of - 1), total - largest - least * (number_of - 1)
    while surplus > 0:
        movable = [i for i in range(1, number_of) if holding[i] < largest] or [i for i in range(1, number_of) if holding[i] < most]
        pool, budget = sum([portions[i] for i in movable]), surplus
        for i in movable:
            addition = min(most - holding[i], max(1, budget * portions[i] // pool), surplus)
            holding[i] = holding[i] + addition
            surplus = surplus - addition
    return np.array(holding)


def gaussian(rng, dims, scale, bound, held_as=jnp.bfloat16):
    drawn = scale * jax.random.normal(rng, dims, jnp.float32)
    return jnp.clip(drawn, min=-bound, max=bound).astype(held_as)


def setup_inputs(seed: int = 0) -> dict:
    seeds = jax.random.split(jax.random.key(seed), 13)
    tokens = draw_tokens(jax.random.fold_in(seeds[12], 71), 0)
    filter_tap_weight = gaussian(seeds[1], (FILTER_TAP_COUNT, C), 0.4, 2.4, jnp.float32)
    norm_gain = jnp.clip(1.0 + 0.1 * jax.random.normal(seeds[2], (C,), jnp.float32), 0.5, 1.5)
    query_weight = draw_query_weight(jax.random.fold_in(seeds[12], 71), 0)
    keyval_weight = draw_keyval_weight(jax.random.fold_in(seeds[12], 71), 0)
    head_weight = gaussian(seeds[5], (HEADS * DV, 2, TRK), (HEADS * DV) ** -0.5, 0.21875)
    head_bias = jnp.clip(jax.random.uniform(seeds[6], (2, TRK), jnp.float32, -1.0, 1.0), -1.0, 1.0)
    exon_start = draw_exon_start(jax.random.fold_in(seeds[12], 71), 0)
    exon_end = draw_exon_end(jax.random.fold_in(seeds[12], 71), 0)
    gene_strand = touch_ends(jax.random.randint(seeds[9], (WINDOWS, GENES), 0, 2), jax.random.fold_in(seeds[9], 1), 0, 1).astype(jnp.int32)
    gene_owner_keys = jax.random.split(jax.random.fold_in(seeds[10], 1), WINDOWS * GENES // GENES)
    gene_owner_turns = jax.random.permutation(jax.random.fold_in(seeds[10], 3), WINDOWS * GENES // GENES)
    gene_owner = jax.vmap(lambda own, number: deal_out(jax.random.fold_in(seeds[10], 2), own, number, GENES, N_BATCH, 1, CAP, 2))(gene_owner_keys, gene_owner_turns).reshape((WINDOWS, GENES, 1))
    gene_target = jnp.clip(4.0 * jax.random.uniform(seeds[11], (N_BATCH, WINDOWS, CAP, TRK), jnp.float32) ** steps_of(seeds[11], (N_BATCH, WINDOWS, CAP, TRK), ((0, 16),), -0.2, 0.2), 0.0, 4.0)
    return dict(tokens=tokens, filter_tap_weight=filter_tap_weight, norm_gain=norm_gain, query_weight=query_weight, keyval_weight=keyval_weight, head_weight=head_weight, head_bias=head_bias, exon_start=exon_start, exon_end=exon_end, gene_strand=gene_strand, gene_owner=gene_owner, gene_target=gene_target)


def as_float(values_in):
    return lax.optimization_barrier(values_in).astype(jnp.float32)

def mix_window(tokens_w, filter_tap_weight, norm_gain):
    dilation_reach_rows = FILTER_TAP_COUNT // 2 * DILATION_STRIDE
    widened = tokens_w.astype(jnp.float32)
    zero_extended = jnp.pad(widened, ((dilation_reach_rows, dilation_reach_rows), (0, 0)))
    tap_total = widened
    for filter_tap_index in range(FILTER_TAP_COUNT):
        tap_total = tap_total + filter_tap_weight[filter_tap_index] * zero_extended[filter_tap_index * DILATION_STRIDE:filter_tap_index * DILATION_STRIDE + WINDOW_BIN_COUNT]
    spread = lax.optimization_barrier(jnp.mean(tap_total * tap_total, axis=-1, keepdims=True))
    return (tap_total * lax.rsqrt(spread + 1e-06) * norm_gain).astype(jnp.bfloat16)

def attend_window(normed, query_weight, keyval_weight):
    queries = jnp.dot(normed, query_weight, preferred_element_type=jnp.float32).astype(jnp.bfloat16)
    keyval = jnp.dot(normed, keyval_weight, preferred_element_type=jnp.float32)
    key_rows = as_float(keyval[:, :DK].astype(jnp.bfloat16))
    value_rows = as_float(keyval[:, DK:].astype(jnp.bfloat16))
    query_blocks = queries.reshape(WINDOW_BIN_COUNT // ROWS, ROWS, HEADS, DK)

    def attend_block(query_block):
        scores = jnp.einsum('qhd,kd->qhk', as_float(query_block), key_rows) * DK ** (-0.5)
        row_max = lax.optimization_barrier(jnp.max(scores, axis=-1, keepdims=True))
        weights = jnp.exp(scores - row_max)
        totals = lax.optimization_barrier(jnp.sum(weights, axis=-1, keepdims=True))
        blended = jnp.einsum('qhk,kd->qhd', as_float(weights.astype(jnp.bfloat16)), value_rows) / totals
        return blended.reshape(ROWS, HEADS * DV).astype(jnp.bfloat16)
    return lax.map(attend_block, query_blocks).reshape(WINDOW_BIN_COUNT, HEADS * DV)

def window_pass(tokens_w, start_w, end_w, strand_w, filter_tap_weight, norm_gain, query_weight, keyval_weight, head_weight, head_bias):
    normed = mix_window(tokens_w, filter_tap_weight, norm_gain)
    attended = attend_window(normed, query_weight, keyval_weight)
    logits = jnp.dot(attended, head_weight.reshape(HEADS * DV, 2 * TRK), preferred_element_type=jnp.float32) + head_bias.reshape(2 * TRK)
    coverage = jax.nn.softplus(logits).astype(jnp.bfloat16).reshape(WINDOW_BIN_COUNT, 2, TRK)
    positions = jnp.arange(WINDOW_BIN_COUNT, dtype=jnp.int32)
    inside = (positions[None, None, :] >= start_w[:, :, None]) & (positions[None, None, :] < end_w[:, :, None])
    counts = lax.optimization_barrier(jnp.sum(inside.astype(jnp.float32), axis=1))
    pooled = jnp.dot(counts, attended.astype(jnp.float32), precision=lax.Precision.HIGHEST)
    length = lax.optimization_barrier(jnp.sum((end_w - start_w).astype(jnp.float32), axis=1))
    pooled = pooled / length[:, None]
    per_strand = jnp.einsum('gh,hst->gst', pooled, head_weight.astype(jnp.float32), precision=lax.Precision.HIGHEST) + head_bias[None]
    gene_logit = jnp.where(strand_w[:, None] == 0, per_strand[:, 0], per_strand[:, 1])
    return (coverage, gene_logit, pooled)

def reference(tokens, filter_tap_weight, norm_gain, query_weight, keyval_weight, head_weight, head_bias, exon_start, exon_end, gene_strand, gene_owner, gene_target):

    def per_window(window_items):
        return window_pass(window_items[0], window_items[1], window_items[2], window_items[3], filter_tap_weight, norm_gain, query_weight, keyval_weight, head_weight, head_bias)
    coverage, gene_logit, pooled = lax.map(per_window, (tokens, exon_start, exon_end, gene_strand))
    owners = gene_owner[:, :, 0]
    gene_index = jnp.arange(GENES, dtype=jnp.int32)
    earlier = (owners[:, :, None] == owners[:, None, :]) & (gene_index[None, None, :] < gene_index[None, :, None])
    slot_rank = lax.optimization_barrier(jnp.sum(earlier.astype(jnp.int32), axis=2))
    window_index = jnp.broadcast_to(jnp.arange(WINDOWS, dtype=jnp.int32)[:, None], (WINDOWS, GENES))
    gene_pred = jnp.zeros((N_BATCH, WINDOWS, CAP, TRK), jnp.float32).at[owners, window_index, slot_rank].set(jax.nn.softplus(gene_logit))
    gene_slope = (jnp.log1p(gene_pred) - gene_target) / (1.0 + gene_pred)
    logit_grad = gene_slope[owners, window_index, slot_rank] * jax.nn.sigmoid(gene_logit)
    strand_plus = jnp.where(gene_strand[:, :, None] == 0, logit_grad, 0.0)
    strand_minus = jnp.where(gene_strand[:, :, None] == 1, logit_grad, 0.0)
    placed = jnp.stack([strand_plus, strand_minus], axis=2)
    head_grad = jnp.einsum('wgh,wgst->hst', pooled, placed, precision=lax.Precision.HIGHEST)
    bias_grad = lax.optimization_barrier(jnp.sum(placed, axis=(0, 1)))
    return (coverage, gene_pred, head_grad, bias_grad)
```

```python
import jax
import jax.numpy as jnp
from jax import lax
from jax.experimental import pallas as pl
from jax.experimental.pallas import tpu as pltpu
from jax.sharding import PartitionSpec as P

HEADS = 4
DK = 128
DV = 192
TRK = 384
TAPS = 5
STRIDE = 64
LOG2E = 1.4426950408889634
BIG = 2.0**100
F32 = jnp.float32
BF16 = jnp.bfloat16
MIB = 1024 * 1024


def whole(shape):
    rank = len(shape)
    return pl.BlockSpec(shape, lambda *grid: (0,) * rank)


def nt_dot(left, right):
    return lax.dot_general(left, right, (((1,), (1,)), ((), ())), preferred_element_type=F32)


def conv_norm(row_blocks, piece, taps_ref, gain_ref, mixed_ref, normed_ref):
    channels = normed_ref.shape[1]
    for n, row_block in enumerate(row_blocks):
        rows = slice(n * STRIDE, (n + 1) * STRIDE)
        squares = jnp.zeros((STRIDE, 128), F32)
        for lane in range(0, channels, 128):
            lanes = slice(lane, lane + 128)
            total = piece(row_block, lanes).astype(F32)
            for k in range(TAPS):
                total = total + taps_ref[k : k + 1, lanes] * piece(
                    row_block + k - TAPS // 2, lanes
                ).astype(F32)
            mixed_ref[rows, lanes] = total
            squares = squares + total * total
        spread = jnp.sum(squares, axis=-1, keepdims=True) / channels
        inverse = lax.rsqrt(spread + 1e-06)
        for lane in range(0, channels, 128):
            lanes = slice(lane, lane + 128)
            normed_ref[rows, lanes] = (mixed_ref[rows, lanes] * inverse * gain_ref[:, lanes]).astype(BF16)


def project(normed_ref, wq_ref, wkv_ref):
    queries = jnp.dot(normed_ref[...], wq_ref[...], preferred_element_type=F32)
    queries = (queries * (DK**-0.5 * LOG2E)).astype(BF16)
    keyval = jnp.dot(normed_ref[...], wkv_ref[...], preferred_element_type=F32).astype(BF16)
    return queries, keyval


def inner_kernel(tok_ref, taps_ref, gain_ref, wq_ref, wkv_ref, q_ref, kv_ref, mixed_ref, normed_ref):
    def piece(block, lanes):
        return tok_ref[block * STRIDE : (block + 1) * STRIDE, lanes]

    conv_norm((2, 3, 4, 5), piece, taps_ref, gain_ref, mixed_ref, normed_ref)
    queries, keyval = project(normed_ref, wq_ref, wkv_ref)
    for h in range(HEADS):
        q_ref[h * 256 : (h + 1) * 256, :] = queries[:, h * DK : (h + 1) * DK]
    kv_ref[0:256, :] = keyval[:, 0:128]
    kv_ref[256:512, :] = keyval[:, 128:256]
    kv_ref[512:640, :] = keyval[128:256, 384:512]
    kv_ref[640:768, :] = keyval[0:128, 256:384]


def edge_kernel(
    tok_ref, low_ref, high_ref, taps_ref, gain_ref, wq_ref, wkv_ref, qi_ref, kvi_ref,
    q_ref, kv_ref, mixed_ref, normed_ref,
):
    def piece(block, lanes):
        if block < 0:
            return low_ref[(block + 2) * STRIDE : (block + 3) * STRIDE, lanes]
        if block >= 8:
            return high_ref[(block - 8) * STRIDE : (block - 7) * STRIDE, lanes]
        return tok_ref[block * STRIDE : (block + 1) * STRIDE, lanes]

    conv_norm((0, 1, 6, 7), piece, taps_ref, gain_ref, mixed_ref, normed_ref)
    queries, keyval = project(normed_ref, wq_ref, wkv_ref)
    for h in range(HEADS):
        lanes = slice(h * DK, (h + 1) * DK)
        q_ref[h * 512 : h * 512 + 128, :] = queries[0:128, lanes]
        q_ref[h * 512 + 128 : h * 512 + 384, :] = qi_ref[h * 256 : (h + 1) * 256, :]
        q_ref[h * 512 + 384 : h * 512 + 512, :] = queries[128:256, lanes]
    for base, column, source in ((0, 0, 0), (512, 128, 256)):
        kv_ref[base : base + 128, :] = keyval[0:128, column : column + 128]
        kv_ref[base + 128 : base + 384, :] = kvi_ref[source : source + 256, :]
        kv_ref[base + 384 : base + 512, :] = keyval[128:256, column : column + 128]
    kv_ref[1024:1152, :] = kvi_ref[512:640, :] + keyval[0:128, 256:384]
    kv_ref[1152:1280, :] = kvi_ref[640:768, :] + keyval[128:256, 384:512]


def front(tokens, low, high, taps, gain, wq, wkv):
    rows, channels = tokens.shape
    scratch = [pltpu.VMEM((256, channels), F32), pltpu.VMEM((256, channels), BF16)]

    def inner(tokens, taps, gain, wq, wkv):
        return pl.pallas_call(
            inner_kernel,
            out_shape=(
                jax.ShapeDtypeStruct((1024, 128), BF16),
                jax.ShapeDtypeStruct((768, 128), BF16),
            ),
            scratch_shapes=scratch,
            compiler_params=pltpu.CompilerParams(vmem_limit_bytes=32 * MIB),
            cost_estimate=pl.CostEstimate(
                flops=2 * 256 * channels * 1024, bytes_accessed=5 * MIB, transcendentals=0
            ),
            name="front_inner",
        )(tokens, taps, gain, wq, wkv)

    q_inner, kv_inner = inner(tokens, taps, gain, wq, wkv)
    return pl.pallas_call(
        edge_kernel,
        out_shape=(
            jax.ShapeDtypeStruct((2048, 128), BF16),
            jax.ShapeDtypeStruct((1280, 128), BF16),
        ),
        scratch_shapes=scratch,
        compiler_params=pltpu.CompilerParams(vmem_limit_bytes=32 * MIB),
        cost_estimate=pl.CostEstimate(
            flops=2 * 256 * channels * 1024, bytes_accessed=6 * MIB, transcendentals=0
        ),
        name="front_edge",
    )(tokens, low, high, taps, gain, wq, wkv, q_inner, kv_inner)


def place_values(kv_ref, base, values_ref, at):
    lane = lax.broadcasted_iota(jnp.int32, (256, 128), 1)
    packed = kv_ref[base + 1024 : base + 1280, :].astype(F32)
    rolled = pltpu.roll(packed, 64, 1)
    one_high = jnp.where(lane == 64, 1.0, 0.0)
    one_low = jnp.where(lane == 0, 1.0, 0.0)
    for parity in range(2):
        values_ref[parity, at : at + 512, 0:128] = kv_ref[base + 512 : base + 1024, :]
    values_ref[0, at : at + 256, 128:256] = jnp.where(lane < 64, packed, one_high).astype(BF16)
    values_ref[0, at + 256 : at + 512, 128:256] = jnp.where(lane < 64, rolled, one_high).astype(BF16)
    values_ref[1, at : at + 256, 128:256] = jnp.where(lane < 64, one_low, rolled).astype(BF16)
    values_ref[1, at + 256 : at + 512, 128:256] = jnp.where(lane < 64, one_low, packed).astype(BF16)


def tile_parity():
    return lax.rem(pl.program_id(0) // 2, 2)


def first_kernel(q_ref, kv_ref, acc_ref, max_ref, values_ref):
    @pl.when(pl.program_id(0) == 0)
    def _():
        place_values(kv_ref, 0, values_ref, 0)

    scores = nt_dot(q_ref[...], kv_ref[0:512, :])
    top = jnp.max(scores, axis=1, keepdims=True)
    weights = jnp.exp2(scores - top).astype(BF16)
    acc_ref[...] = jnp.dot(weights, values_ref[tile_parity()], preferred_element_type=F32)
    max_ref[...] = jnp.broadcast_to(top, max_ref.shape)


def add_blocks(q_ref, top, acc, kv_refs, values_ref):
    parity = tile_parity()
    for n, kv_ref in enumerate(kv_refs):
        scores = nt_dot(q_ref[...], kv_ref[0:512, :])
        weights = jnp.exp2(scores - top).astype(BF16)
        acc = acc + jnp.dot(
            weights, values_ref[parity, n * 512 : (n + 1) * 512, :], preferred_element_type=F32
        )
    return acc


def more_kernel(q_ref, max_ref, acc_in_ref, *rest):
    kv_refs, (acc_ref, values_ref) = rest[:-2], rest[-2:]

    @pl.when(pl.program_id(0) == 0)
    def _():
        for n, kv_ref in enumerate(kv_refs):
            place_values(kv_ref, 0, values_ref, n * 512)

    acc_ref[...] = add_blocks(q_ref, max_ref[:, 0:1], acc_in_ref[...], kv_refs, values_ref)


def last_kernel(block_count, q_ref, max_ref, acc_in_ref, cnt_ref, inv_len_ref, *rest):
    kv_refs, rest = rest[:block_count], rest[block_count:]
    every_ref, rest = rest[:16], rest[16:]
    att_ref, pool_ref, values_ref, acc_ref, held_ref, slow_values_ref, top_ref = rest
    step = pl.program_id(0)
    head, half, parity = step // 2, lax.rem(step, 2), tile_parity()

    @pl.when(step == 0)
    def _():
        for n, kv_ref in enumerate(kv_refs):
            place_values(kv_ref, 0, values_ref, n * 512)

    acc_ref[...] = add_blocks(q_ref, max_ref[:, 0:1], acc_in_ref[...], kv_refs, values_ref)

    def totals():
        return jnp.where(parity == 0, acc_ref[:, 192:193], acc_ref[:, 128:129])

    outside = jnp.sum(jnp.where(totals() < BIG, 0.0, 1.0))

    @pl.when(outside > 0.0)
    def _():
        for n, every in enumerate(every_ref):
            pltpu.sync_copy(every, held_ref.at[pl.ds(n * 1280, 1280)])
        acc_ref[...] = jnp.zeros_like(acc_ref)
        top_ref[...] = jnp.full_like(top_ref, -jnp.inf)

        def one_block(n, carry):
            base = pl.multiple_of(n * 1280, 1280)
            block = held_ref.at[pl.ds(base, 1280)]
            place_values(block, 0, slow_values_ref, 0)
            scores = nt_dot(q_ref[...], block[0:512, :])
            before = top_ref[:, 0:1]
            top = jnp.maximum(before, jnp.max(scores, axis=1, keepdims=True))
            weights = jnp.exp2(scores - top).astype(BF16)
            acc_ref[...] = acc_ref[...] * jnp.exp2(before - top) + jnp.dot(
                weights, slow_values_ref[parity], preferred_element_type=F32
            )
            top_ref[...] = jnp.broadcast_to(top, top_ref.shape)
            return carry

        lax.fori_loop(0, 16, one_block, 0)

    scaled = (acc_ref[...] * (1.0 / totals())).astype(BF16)
    rows = pl.ds(pl.multiple_of(half * 256, 256), 256)
    att_ref[rows, pl.ds(pl.multiple_of(head * 128, 128), 128)] = scaled[:, 0:128]
    pair = pl.ds(pl.multiple_of(512 + (head // 2) * 128, 128), 128)
    lane = lax.broadcasted_iota(jnp.int32, (256, 128), 1)

    @pl.when(parity == 0)
    def _():
        att_ref[rows, pair] = scaled[:, 128:256]

    @pl.when(parity == 1)
    def _():
        att_ref[rows, pair] = jnp.where(lane < 64, att_ref[rows, pair], scaled[:, 128:256])

    @pl.when(step == 2 * HEADS - 1)
    def _():
        pool = jnp.dot(cnt_ref[...], att_ref[...], preferred_element_type=F32)
        pool_ref[...] = (pool * inv_len_ref[...]).astype(BF16)


TILE = lambda width: pl.BlockSpec((256, width), lambda t: (t, 0))
BLOCK = (1280, 128)


def attend_cost(blocks):
    return pl.CostEstimate(
        flops=blocks * 2048 * 512 * 2 * 512,
        bytes_accessed=6 * MIB,
        transcendentals=blocks * 2048 * 512,
    )


def attend_first(q, kv):
    return pl.pallas_call(
        first_kernel,
        grid=(8,),
        in_specs=[TILE(128), whole(BLOCK)],
        out_specs=(TILE(256), TILE(128)),
        out_shape=(jax.ShapeDtypeStruct((2048, 256), F32), jax.ShapeDtypeStruct((2048, 128), F32)),
        scratch_shapes=[pltpu.VMEM((2, 512, 256), BF16)],
        compiler_params=pltpu.CompilerParams(vmem_limit_bytes=24 * MIB),
        cost_estimate=attend_cost(1),
        name="attend_first",
    )(q, kv)


def attend_more(q, top, acc, blocks):
    count = len(blocks)
    return pl.pallas_call(
        more_kernel,
        grid=(8,),
        in_specs=[TILE(128), TILE(128), TILE(256)] + [whole(BLOCK)] * count,
        out_specs=TILE(256),
        out_shape=jax.ShapeDtypeStruct((2048, 256), F32),
        scratch_shapes=[pltpu.VMEM((2, 512 * count, 256), BF16)],
        input_output_aliases={2: 0},
        compiler_params=pltpu.CompilerParams(vmem_limit_bytes=24 * MIB),
        cost_estimate=attend_cost(count),
        name="attend_more",
    )(q, top, acc, *blocks)


def attend_last(q, top, acc, counts, inv_len, blocks, every):
    count = len(blocks)

    def kernel(*refs):
        last_kernel(count, *refs)

    return pl.pallas_call(
        kernel,
        grid=(8,),
        in_specs=[TILE(128), TILE(128), TILE(256), whole((32, 512)), whole((32, 1))]
        + [whole(BLOCK)] * count
        + [pl.BlockSpec(memory_space=pl.ANY)] * len(every),
        out_specs=(whole((512, 768)), whole((32, 768))),
        out_shape=(jax.ShapeDtypeStruct((512, 768), BF16), jax.ShapeDtypeStruct((32, 768), BF16)),
        scratch_shapes=[
            pltpu.VMEM((2, 512 * count, 256), BF16),
            pltpu.VMEM((256, 256), F32),
            pltpu.VMEM((16 * 1280, 128), BF16),
            pltpu.VMEM((2, 512, 256), BF16),
            pltpu.VMEM((256, 128), F32),
        ],
        compiler_params=pltpu.CompilerParams(vmem_limit_bytes=32 * MIB),
        cost_estimate=attend_cost(count),
        name="attend_last",
    )(q, top, acc, counts, inv_len, *blocks, *every)


def soft_plus(x):
    return jnp.maximum(x, 0.0) + jnp.log1p(jnp.exp(-jnp.abs(x)))


def coverage_kernel(att_ref, weight_ref, bias_ref, out_ref):
    logits = jnp.dot(att_ref[...], weight_ref[...], preferred_element_type=F32) + bias_ref[...]
    out_ref[...] = soft_plus(logits).astype(BF16)


def coverage_of(att, weight, bias):
    return pl.pallas_call(
        coverage_kernel,
        grid=(4,),
        in_specs=[pl.BlockSpec((128, 768), lambda t: (t, 0)), whole((768, 768)), whole((1, 768))],
        out_specs=pl.BlockSpec((128, 768), lambda t: (t, 0)),
        out_shape=jax.ShapeDtypeStruct((512, 768), BF16),
        compiler_params=pltpu.CompilerParams(vmem_limit_bytes=16 * MIB),
        cost_estimate=pl.CostEstimate(
            flops=2 * 512 * 768 * 768, bytes_accessed=3 * MIB, transcendentals=512 * 768 * 2
        ),
        name="coverage",
    )(att, weight, bias)


def tail_kernel(
    place_ref, a_ref, b_ref, c_ref, d_ref, weight_ref, bias_ref, target_ref, strand_ref, sel_ref,
    pred_ref, head_ref, bias_grad_ref, pooled_ref, hold_ref,
):
    for n, ref in enumerate((a_ref, b_ref, c_ref, d_ref)):
        for j in range(4):
            at = pl.multiple_of(place_ref[n] + place_ref[4 + j], 32)
            pooled_ref[pl.ds(at, 32), :] = ref[j * 32 : (j + 1) * 32, :]
    pooled = pooled_ref[...]
    logits = jnp.dot(pooled, weight_ref[...], preferred_element_type=F32) + bias_ref[...]
    plus = strand_ref[...] < 0.5
    logit = jnp.where(plus, logits[:, 0:TRK], logits[:, TRK : 2 * TRK])
    decay = jnp.exp(-jnp.abs(logit))
    pred = jnp.maximum(logit, 0.0) + jnp.log1p(decay)
    slope = (jnp.log1p(pred) - target_ref[...].astype(F32)) / (1.0 + pred)
    grad = slope * (jnp.where(logit >= 0.0, 1.0, decay) / (1.0 + decay))
    pred_ref[...] = jnp.dot(sel_ref[...], pred.astype(BF16), preferred_element_type=F32)
    for strand in range(2):
        placed = jnp.where(plus == (strand == 0), grad, 0.0)
        bias_grad_ref[strand : strand + 1, :] = jnp.sum(placed, axis=0, keepdims=True)
        hold_ref[:, strand * TRK : (strand + 1) * TRK] = placed.astype(BF16)
    head = lax.dot_general(pooled, hold_ref[...], (((0,), (0,)), ((), ())), preferred_element_type=F32)
    for h in range(HEADS):
        head_ref[h * DV : h * DV + 128, :] = head[h * 128 : (h + 1) * 128, :]
        head_ref[h * DV + 128 : (h + 1) * DV, :] = head[512 + h * 64 : 512 + (h + 1) * 64, :]


def tail(place, parts, weight, bias, target, strand, sel):
    vmem = pl.BlockSpec(memory_space=pltpu.VMEM)
    return pl.pallas_call(
        tail_kernel,
        in_specs=[pl.BlockSpec(memory_space=pltpu.SMEM)] + [vmem] * 9,
        out_specs=(vmem, vmem, vmem),
        out_shape=(
            jax.ShapeDtypeStruct((64, TRK), F32),
            jax.ShapeDtypeStruct((768, 2 * TRK), F32),
            jax.ShapeDtypeStruct((2, TRK), F32),
        ),
        scratch_shapes=[pltpu.VMEM((512, 768), BF16), pltpu.VMEM((512, 768), BF16)],
        compiler_params=pltpu.CompilerParams(vmem_limit_bytes=32 * MIB),
        cost_estimate=pl.CostEstimate(
            flops=4 * 512 * 768 * 768, bytes_accessed=6 * MIB, transcendentals=512 * 384 * 4
        ),
        name="tail",
    )(place, *parts, weight, bias, target, strand, sel)


def permute(array, axis, target):
    count = lax.axis_size(axis)
    return lax.ppermute(array, axis, [(i, target(i)) for i in range(count)])


def z_up(s):
    return s // 8 * 8 + (s + 1) % 8


def z_down(s):
    return s // 8 * 8 + (s + 7) % 8


def y_over(s):
    return s ^ 8


def permuted_rows(weight):
    first = [weight[h * DV : h * DV + 128] for h in range(HEADS)]
    rest = [weight[h * DV + 128 : (h + 1) * DV] for h in range(HEADS)]
    return jnp.concatenate(first + rest, axis=0)


def window_order(array):
    split = array.reshape((2, 4, 2) + array.shape[1:])
    return jnp.swapaxes(split, 1, 2).reshape(array.shape)


def gene_tables(gene_target, gene_owner, gene_strand):
    genes = gene_strand.shape[1]
    code = (gene_owner[0, :, 0] * 2 + gene_strand[0]).astype(BF16)
    code_rows = jnp.pad(code[None], ((0, 15), (0, TRK - genes)))
    mine = jnp.concatenate([gene_target[0].reshape(64, TRK).astype(BF16), code_rows], axis=0)
    table = lax.all_gather(mine, "batch", axis=0, tiled=False)
    codes = window_order(table[:, 64, :genes].astype(jnp.int32))
    owners, strands = codes // 2, codes % 2
    gene = jnp.arange(genes, dtype=jnp.int32)
    earlier = (owners[:, :, None] == owners[:, None, :]) & (gene[None, None, :] < gene[None, :, None])
    rank = jnp.sum(earlier.astype(jnp.int32), axis=2)
    slot = owners * 4 + rank
    targets = jnp.swapaxes(table[:, :64].reshape(16, 16, 4, TRK), 0, 1).reshape(16, 64, TRK)
    targets = window_order(targets)
    chosen = (slot[:, :, None] == jnp.arange(64, dtype=jnp.int32)).astype(BF16)
    target = jnp.einsum("wgs,wst->wgt", chosen, targets, preferred_element_type=F32)
    target = target.astype(BF16).reshape(16 * genes, TRK)
    window = window_order(jnp.arange(16, dtype=jnp.int32))
    wanted = window[:, None] * 4 + rank
    wanted = jnp.where(owners == lax.axis_index("batch"), wanted, -1).reshape(1, 16 * genes)
    sel = (jnp.arange(64, dtype=jnp.int32)[:, None] == wanted).astype(BF16)
    return target, strands.reshape(16 * genes, 1).astype(F32), sel


def local(
    tokens,
    filter_tap_weight,
    norm_gain,
    query_weight,
    keyval_weight,
    head_weight,
    head_bias,
    exon_start,
    exon_end,
    gene_strand,
    gene_owner,
    gene_target,
):
    rows = tokens[0]
    row_count = rows.shape[0]
    reach = TAPS // 2 * STRIDE
    low = lax.ppermute(rows[row_count - reach :], "seq", [(i, i + 1) for i in range(15)])
    high = lax.ppermute(rows[:reach], "seq", [(i + 1, i) for i in range(15)])
    value_rest = keyval_weight[:, 256:320]
    blank = jnp.zeros_like(value_rest)
    wkv = jnp.concatenate([keyval_weight[:, :256], value_rest, blank, blank, value_rest], axis=1)
    q, own = front(rows, low, high, filter_tap_weight, norm_gain[None], query_weight, wkv)

    target, strand, sel = gene_tables(gene_target, gene_owner, gene_strand)
    positions = lax.axis_index("seq") * row_count + jnp.arange(row_count, dtype=jnp.int32)
    starts, stops = exon_start[0], exon_end[0]
    inside = (positions >= starts[:, :, None]) & (positions < stops[:, :, None])
    counts = jnp.sum(inside.astype(F32), axis=1).astype(BF16)
    inv_len = 1.0 / jnp.sum((stops - starts).astype(F32), axis=1, keepdims=True)
    weight = permuted_rows(head_weight.reshape(HEADS * DV, 2 * TRK))
    bias = head_bias.reshape(1, 2 * TRK)

    def up(x):
        return permute(x, "seq", z_up)

    def down(x):
        return permute(x, "seq", z_down)

    up1, down1 = up(own), down(own)
    over0 = permute(own, "seq", y_over)
    up2, down2 = up(up1), down(down1)
    over_up1, over_down1 = up(over0), down(over0)
    up3, down3 = up(up2), down(down2)
    over_up2, over_down2 = up(over_up1), down(over_down1)
    up4 = up(up3)
    over_up3, over_down3 = up(over_up2), down(over_down2)
    over_down4 = down(over_down3)
    acc, top = attend_first(q, own)
    acc = attend_more(q, top, acc, [up1, down1, over0])
    acc = attend_more(q, top, acc, [up2, down2, over_up1, over_down1])
    acc = attend_more(q, top, acc, [up3, down3, over_up2, over_down2])
    acc = attend_more(q, top, acc, [up4, over_up3])
    every = [own, up1, down1, over0, up2, down2, over_up1, over_down1, up3, down3, over_up2,
             over_down2, up4, over_up3, over_down3, over_down4]
    att, pool = attend_last(q, top, acc, counts, inv_len, [over_down3, over_down4], every)

    coverage = coverage_of(att, weight, bias).reshape(1, row_count, 2, TRK)

    def join(x, axis, masks):
        a, b, c = [permute(x, axis, lambda s, m=m: s ^ m) for m in masks]
        return a, b, c

    for masks in ((1, 8, 9), (2, 4, 6)):
        a, b, c = [piece.astype(F32) for piece in join(pool, "seq", masks)]
        pool = ((pool.astype(F32) + a) + (b + c)).astype(BF16)
    gathered = jnp.concatenate([pool, *join(pool, "batch", (2, 4, 6))], axis=0)
    other_y = permute(gathered, "batch", lambda s: s ^ 8)
    other_core = permute(gathered, "batch", lambda s: s ^ 1)
    other_both = permute(other_y, "batch", lambda s: s ^ 1)
    me = lax.axis_index("batch")
    y, x, core = me // 8, me // 2 % 4, me % 2
    place = jnp.stack(
        [
            (y * 2 + core) * 128,
            ((1 - y) * 2 + core) * 128,
            (y * 2 + 1 - core) * 128,
            ((1 - y) * 2 + 1 - core) * 128,
            x * 32,
            (x ^ 1) * 32,
            (x ^ 2) * 32,
            (x ^ 3) * 32,
        ]
    ).astype(jnp.int32)
    pred, head_grad, bias_grad = tail(
        place, (gathered, other_y, other_core, other_both), weight, bias, target, strand, sel
    )
    return (
        coverage,
        pred.reshape(1, 16, 4, TRK),
        head_grad.reshape(HEADS * DV, 2, TRK),
        bias_grad,
    )


def solution(mesh):
    in_specs = (
        P("batch", "seq", None),
        P(),
        P(),
        P(),
        P(),
        P(),
        P(),
        P("batch", None, None),
        P("batch", None, None),
        P("batch", None),
        P("batch", None, None),
        P("batch", None, None, None),
    )
    out_specs = (P("batch", "seq", None, None), P("batch", None, None, None), P(), P())
    return jax.shard_map(local, mesh=mesh, in_specs=in_specs, out_specs=out_specs, check_vma=False)
```

```python
import jax
import jax.numpy as jnp
from jax import lax
from jax.experimental import pallas as pl
from jax.experimental.pallas import tpu as pltpu
from jax.sharding import PartitionSpec as P

HEADS = 4
DK = 128
DV = 192
TRK = 384
TAPS = 5
STRIDE = 64
LOG2E = 1.4426950408889634
BIG = 2.0**100
F32 = jnp.float32
BF16 = jnp.bfloat16
MIB = 1024 * 1024
VMEM = pl.BlockSpec(memory_space=pltpu.VMEM)


def whole(shape):
    rank = len(shape)
    return pl.BlockSpec(shape, lambda *grid: (0,) * rank)


def nt_dot(left, right):
    return lax.dot_general(left, right, (((1,), (1,)), ((), ())), preferred_element_type=F32)


def conv_norm(row_blocks, piece, taps_ref, gain_ref, mixed_ref, normed_ref):
    channels = normed_ref.shape[1]
    for n, row_block in enumerate(row_blocks):
        rows = slice(n * STRIDE, (n + 1) * STRIDE)
        squares = jnp.zeros((STRIDE, 128), F32)
        for lane in range(0, channels, 128):
            lanes = slice(lane, lane + 128)
            total = piece(row_block, lanes).astype(F32)
            for k in range(TAPS):
                total = total + taps_ref[k : k + 1, lanes] * piece(
                    row_block + k - TAPS // 2, lanes
                ).astype(F32)
            mixed_ref[rows, lanes] = total
            squares = squares + total * total
        spread = jnp.sum(squares, axis=-1, keepdims=True) / channels
        inverse = lax.rsqrt(spread + 1e-06)
        for lane in range(0, channels, 128):
            lanes = slice(lane, lane + 128)
            normed_ref[rows, lanes] = (mixed_ref[rows, lanes] * inverse * gain_ref[:, lanes]).astype(BF16)


def project(normed_ref, wq_ref, wkv_ref, wide_ref):
    wide_ref[...] = jnp.zeros_like(wide_ref)
    wide_ref[0:64, :] = wkv_ref[256:320, :]
    wide_ref[192:256, :] = wkv_ref[256:320, :]
    queries = jnp.dot(normed_ref[...], wq_ref[...], preferred_element_type=F32)
    queries = (queries * (DK**-0.5 * LOG2E)).astype(BF16)
    first = nt_dot(normed_ref[...], wkv_ref[0:256, :]).astype(BF16)
    rest = nt_dot(normed_ref[...], wide_ref[...]).astype(BF16)
    return queries, first, rest


def inner_kernel(tok_ref, taps_ref, gain_ref, wq_ref, wkv_ref, q_ref, kv_ref, mixed_ref, normed_ref, wide_ref):
    def piece(block, lanes):
        return tok_ref[block * STRIDE : (block + 1) * STRIDE, lanes]

    conv_norm((2, 3, 4, 5), piece, taps_ref, gain_ref, mixed_ref, normed_ref)
    queries, first, rest = project(normed_ref, wq_ref, wkv_ref, wide_ref)
    for h in range(HEADS):
        q_ref[h * 256 : (h + 1) * 256, :] = queries[:, h * DK : (h + 1) * DK]
    kv_ref[0:256, :] = first[:, 0:128]
    kv_ref[256:512, :] = first[:, 128:256]
    kv_ref[512:640, :] = rest[128:256, 128:256]
    kv_ref[640:768, :] = rest[0:128, 0:128]


def edge_kernel(
    tok_ref, low_ref, high_ref, taps_ref, gain_ref, wq_ref, wkv_ref, qi_ref, kvi_ref,
    q_ref, kv_ref, mixed_ref, normed_ref, wide_ref,
):
    def piece(block, lanes):
        if block < 0:
            return low_ref[(block + 2) * STRIDE : (block + 3) * STRIDE, lanes]
        if block >= 8:
            return high_ref[(block - 8) * STRIDE : (block - 7) * STRIDE, lanes]
        return tok_ref[block * STRIDE : (block + 1) * STRIDE, lanes]

    conv_norm((0, 1, 6, 7), piece, taps_ref, gain_ref, mixed_ref, normed_ref)
    queries, first, rest = project(normed_ref, wq_ref, wkv_ref, wide_ref)
    for h in range(HEADS):
        lanes = slice(h * DK, (h + 1) * DK)
        q_ref[h * 512 : h * 512 + 128, :] = queries[0:128, lanes]
        q_ref[h * 512 + 128 : h * 512 + 384, :] = qi_ref[h * 256 : (h + 1) * 256, :]
        q_ref[h * 512 + 384 : h * 512 + 512, :] = queries[128:256, lanes]
    for base, column, source in ((0, 0, 0), (512, 128, 256)):
        kv_ref[base : base + 128, :] = first[0:128, column : column + 128]
        kv_ref[base + 128 : base + 384, :] = kvi_ref[source : source + 256, :]
        kv_ref[base + 384 : base + 512, :] = first[128:256, column : column + 128]
    kv_ref[1024:1152, :] = kvi_ref[512:640, :] + rest[0:128, 0:128]
    kv_ref[1152:1280, :] = kvi_ref[640:768, :] + rest[128:256, 128:256]


def front(tokens, low, high, taps, gain, wq, wkv):
    rows, channels = tokens.shape
    scratch = [pltpu.VMEM((256, channels), F32), pltpu.VMEM((256, channels), BF16)]
    scratch += [pltpu.VMEM((256, channels), BF16)]

    def inner(tokens, taps, gain, wq, wkv):
        return pl.pallas_call(
            inner_kernel,
            out_shape=(
                jax.ShapeDtypeStruct((1024, 128), BF16),
                jax.ShapeDtypeStruct((768, 128), BF16),
            ),
            in_specs=[VMEM] * 5,
            out_specs=(VMEM, VMEM),
            scratch_shapes=scratch,
            compiler_params=pltpu.CompilerParams(vmem_limit_bytes=8 * MIB),
            cost_estimate=pl.CostEstimate(
                flops=2 * 256 * channels * 1024, bytes_accessed=5 * MIB, transcendentals=0
            ),
            name="front_inner",
        )(tokens, taps, gain, wq, wkv)

    q_inner, kv_inner = inner(tokens, taps, gain, wq, wkv)
    operands = (tokens, low, high, taps, gain, wq, wkv, q_inner, kv_inner)
    return pl.pallas_call(
        edge_kernel,
        in_specs=[VMEM] * len(operands),
        out_specs=(VMEM, VMEM),
        out_shape=(
            jax.ShapeDtypeStruct((2048, 128), BF16),
            jax.ShapeDtypeStruct((1280, 128), BF16),
        ),
        scratch_shapes=scratch,
        compiler_params=pltpu.CompilerParams(vmem_limit_bytes=8 * MIB),
        cost_estimate=pl.CostEstimate(
            flops=2 * 256 * channels * 1024, bytes_accessed=6 * MIB, transcendentals=0
        ),
        name="front_edge",
    )(*operands)


def place_values(kv_ref, base, values_ref, at):
    lane = lax.broadcasted_iota(jnp.int32, (256, 128), 1)
    packed = kv_ref[base + 1024 : base + 1280, :].astype(F32)
    rolled = pltpu.roll(packed, 64, 1)
    one_high = jnp.where(lane == 64, 1.0, 0.0)
    one_low = jnp.where(lane == 0, 1.0, 0.0)
    for parity in range(2):
        values_ref[parity, at : at + 512, 0:128] = kv_ref[base + 512 : base + 1024, :]
    values_ref[0, at : at + 256, 128:256] = jnp.where(lane < 64, packed, one_high).astype(BF16)
    values_ref[0, at + 256 : at + 512, 128:256] = jnp.where(lane < 64, rolled, one_high).astype(BF16)
    values_ref[1, at : at + 256, 128:256] = jnp.where(lane < 64, one_low, rolled).astype(BF16)
    values_ref[1, at + 256 : at + 512, 128:256] = jnp.where(lane < 64, one_low, packed).astype(BF16)


def rows_of(head):
    return pl.ds(pl.multiple_of(head * 512, 512), 512)


def each_pair(body):
    def step(pair, carry):
        for parity in range(2):
            body(pair, parity)
        return carry

    lax.fori_loop(0, HEADS // 2, step, 0)


def first_kernel(q_ref, kv_ref, acc_ref, max_ref, values_ref):
    place_values(kv_ref, 0, values_ref, 0)

    def one_head(pair, parity):
        rows = rows_of(pair * 2 + parity)
        scores = nt_dot(q_ref[rows, :], kv_ref[0:512, :])
        top = jnp.max(scores, axis=1, keepdims=True)
        weights = jnp.exp2(scores - top).astype(BF16)
        acc_ref[rows, :] = jnp.dot(weights, values_ref[parity], preferred_element_type=F32)
        max_ref[rows, :] = jnp.broadcast_to(top, (512, 128))

    each_pair(one_head)


def add_blocks(pair, parity, q_ref, max_ref, acc_ref, kv_refs, values_ref):
    rows = rows_of(pair * 2 + parity)
    queries, top, acc = q_ref[rows, :], max_ref[rows, 0:1], acc_ref[rows, :]
    for n, kv_ref in enumerate(kv_refs):
        scores = nt_dot(queries, kv_ref[0:512, :])
        weights = jnp.exp2(scores - top).astype(BF16)
        acc = acc + jnp.dot(
            weights, values_ref[parity, n * 512 : (n + 1) * 512, :], preferred_element_type=F32
        )
    return acc


def more_kernel(q_ref, max_ref, acc_in_ref, *rest):
    kv_refs, (acc_ref, values_ref) = rest[:-2], rest[-2:]
    for n, kv_ref in enumerate(kv_refs):
        place_values(kv_ref, 0, values_ref, n * 512)

    def one_head(pair, parity):
        acc_ref[rows_of(pair * 2 + parity), :] = add_blocks(
            pair, parity, q_ref, max_ref, acc_in_ref, kv_refs, values_ref
        )

    each_pair(one_head)


def last_kernel(block_count, q_ref, max_ref, acc_in_ref, cnt_ref, inv_len_ref, *rest):
    kv_refs, rest = rest[:block_count], rest[block_count:]
    all_q_ref, every_ref, rest = rest[0], rest[1:17], rest[17:]
    att_ref, pool_ref, values_ref, outside_ref, held_q_ref, held_ref, slow_values_ref, acc_ref = rest
    lane = lax.broadcasted_iota(jnp.int32, (512, 128), 1)
    outside_ref[...] = jnp.zeros_like(outside_ref)
    for n, kv_ref in enumerate(kv_refs):
        place_values(kv_ref, 0, values_ref, n * 512)

    def finish(pair, accs):
        totals = accs[0][:, 192:193], accs[1][:, 128:129]
        even, odd = [(acc * (1.0 / total)).astype(BF16) for acc, total in zip(accs, totals)]
        at = [pl.multiple_of(column, 128) for column in (pair * 256, pair * 256 + 128, pair * 128 + 512)]
        att_ref[:, pl.ds(at[0], 128)] = even[:, 0:128]
        att_ref[:, pl.ds(at[1], 128)] = odd[:, 0:128]
        att_ref[:, pl.ds(at[2], 128)] = jnp.where(lane < 64, even[:, 128:256], odd[:, 128:256])
        return totals

    def one_pair(pair, carry):
        accs = [
            add_blocks(pair, parity, q_ref, max_ref, acc_in_ref, kv_refs, values_ref)
            for parity in range(2)
        ]
        for total in finish(pair, accs):
            outside_ref[...] = outside_ref[...] + jnp.where(total < BIG, 0.0, 1.0)
        return carry

    lax.fori_loop(0, HEADS // 2, one_pair, 0)

    @pl.when(jnp.sum(outside_ref[...]) > 0.0)
    def _():
        pltpu.sync_copy(all_q_ref, held_q_ref)
        for n, every in enumerate(every_ref):
            pltpu.sync_copy(every, held_ref.at[pl.ds(n * 1280, 1280)])

        def redo_head(pair, parity):
            queries = held_q_ref[rows_of(pair * 2 + parity), :]
            acc_ref[parity] = jnp.zeros((512, 256), F32)

            def one_block(n, before):
                block = held_ref.at[pl.ds(pl.multiple_of(n * 1280, 1280), 1280)]
                place_values(block, 0, slow_values_ref, 0)
                scores = nt_dot(queries, block[0:512, :])
                top = jnp.maximum(before, jnp.max(scores, axis=1, keepdims=True))
                weights = jnp.exp2(scores - top).astype(BF16)
                acc_ref[parity] = acc_ref[parity] * jnp.exp2(before - top) + jnp.dot(
                    weights, slow_values_ref[parity], preferred_element_type=F32
                )
                return top

            lax.fori_loop(0, 16, one_block, jnp.full((512, 1), -jnp.inf, F32))

        def redo_pair(pair, carry):
            for parity in range(2):
                redo_head(pair, parity)
            finish(pair, (acc_ref[0], acc_ref[1]))
            return carry

        lax.fori_loop(0, HEADS // 2, redo_pair, 0)

    pool = jnp.dot(cnt_ref[...], att_ref[...], preferred_element_type=F32)
    pool_ref[...] = (pool * inv_len_ref[...]).astype(BF16)


def attend_cost(blocks):
    return pl.CostEstimate(
        flops=blocks * 2048 * 512 * 2 * 512,
        bytes_accessed=6 * MIB,
        transcendentals=blocks * 2048 * 512,
    )


def attend_first(q, kv):
    return pl.pallas_call(
        first_kernel,
        in_specs=[VMEM, VMEM],
        out_specs=(VMEM, VMEM),
        out_shape=(jax.ShapeDtypeStruct((2048, 256), F32), jax.ShapeDtypeStruct((2048, 128), F32)),
        scratch_shapes=[pltpu.VMEM((2, 512, 256), BF16)],
        compiler_params=pltpu.CompilerParams(vmem_limit_bytes=8 * MIB),
        cost_estimate=attend_cost(1),
        name="attend_first",
    )(q, kv)


def attend_more(q, top, acc, blocks):
    count = len(blocks)
    return pl.pallas_call(
        more_kernel,
        in_specs=[VMEM] * (3 + count),
        out_specs=VMEM,
        out_shape=jax.ShapeDtypeStruct((2048, 256), F32),
        scratch_shapes=[pltpu.VMEM((2, 512 * count, 256), BF16)],
        input_output_aliases={2: 0},
        compiler_params=pltpu.CompilerParams(vmem_limit_bytes=8 * MIB),
        cost_estimate=attend_cost(count),
        name="attend_more",
    )(q, top, acc, *blocks)


def attend_last(q, top, acc, counts, inv_len, blocks, every):
    count = len(blocks)

    def kernel(*refs):
        last_kernel(count, *refs)

    return pl.pallas_call(
        kernel,
        in_specs=[VMEM] * (5 + count) + [pl.BlockSpec(memory_space=pl.ANY)] * (1 + len(every)),
        out_specs=(VMEM, VMEM),
        out_shape=(jax.ShapeDtypeStruct((512, 768), BF16), jax.ShapeDtypeStruct((32, 768), BF16)),
        scratch_shapes=[
            pltpu.VMEM((2, 512 * count, 256), BF16),
            pltpu.VMEM((512, 1), F32),
            pltpu.VMEM((2048, 128), BF16),
            pltpu.VMEM((16 * 1280, 128), BF16),
            pltpu.VMEM((2, 512, 256), BF16),
            pltpu.VMEM((2, 512, 256), F32),
        ],
        compiler_params=pltpu.CompilerParams(vmem_limit_bytes=16 * MIB),
        cost_estimate=attend_cost(count),
        name="attend_last",
    )(q, top, acc, counts, inv_len, *blocks, q, *every)


def soft_plus(x):
    return jnp.maximum(x, 0.0) + jnp.log1p(jnp.exp(-jnp.abs(x)))


def order_rows(weight_ref, ordered_ref):
    for h in range(HEADS):
        ordered_ref[h * 128 : (h + 1) * 128, :] = weight_ref[h * DV : h * DV + 128, :]
        ordered_ref[512 + h * 64 : 512 + (h + 1) * 64, :] = weight_ref[h * DV + 128 : (h + 1) * DV, :]


def coverage_kernel(att_ref, weight_ref, bias_ref, out_ref, ordered_ref):
    order_rows(weight_ref, ordered_ref)

    def step(n, carry):
        rows = pl.ds(pl.multiple_of(n * 128, 128), 128)
        logits = jnp.dot(att_ref[rows, :], ordered_ref[...], preferred_element_type=F32)
        out_ref[rows, :] = soft_plus(logits + bias_ref[...]).astype(BF16)
        return carry

    lax.fori_loop(0, 4, step, 0)


def coverage_of(att, weight, bias):
    return pl.pallas_call(
        coverage_kernel,
        in_specs=[VMEM] * 3,
        out_specs=VMEM,
        out_shape=jax.ShapeDtypeStruct((512, 768), BF16),
        scratch_shapes=[pltpu.VMEM((768, 768), BF16)],
        compiler_params=pltpu.CompilerParams(vmem_limit_bytes=8 * MIB),
        cost_estimate=pl.CostEstimate(
            flops=2 * 512 * 768 * 768, bytes_accessed=3 * MIB, transcendentals=512 * 768 * 2
        ),
        name="coverage",
    )(att, weight, bias)


def tail_kernel(
    place_ref, a_ref, b_ref, c_ref, d_ref, weight_ref, bias_ref, target_ref, strand_ref, sel_ref,
    pred_ref, head_ref, bias_grad_ref, pooled_ref, hold_ref, ordered_ref,
):
    order_rows(weight_ref, ordered_ref)
    for n, ref in enumerate((a_ref, b_ref, c_ref, d_ref)):
        for j in range(4):
            at = pl.multiple_of(place_ref[n] + place_ref[4 + j], 32)
            pooled_ref[pl.ds(at, 32), :] = ref[j * 32 : (j + 1) * 32, :]
    pooled = pooled_ref[...]
    logits = jnp.dot(pooled, ordered_ref[...], preferred_element_type=F32) + bias_ref[...]
    plus = strand_ref[:, 0:1] < 0.5
    logit = jnp.where(plus, logits[:, 0:TRK], logits[:, TRK : 2 * TRK])
    decay = jnp.exp(-jnp.abs(logit))
    pred = jnp.maximum(logit, 0.0) + jnp.log1p(decay)
    slope = (jnp.log1p(pred) - target_ref[...].astype(F32)) / (1.0 + pred)
    grad = slope * (jnp.where(logit >= 0.0, 1.0, decay) / (1.0 + decay))
    pred_ref[...] = lax.dot_general(
        sel_ref[...], pred.astype(BF16), (((0,), (0,)), ((), ())), preferred_element_type=F32
    )[0:64]
    for strand in range(2):
        placed = jnp.where(plus == (strand == 0), grad, 0.0)
        bias_grad_ref[strand : strand + 1, :] = jnp.sum(placed, axis=0, keepdims=True)
        hold_ref[:, strand * TRK : (strand + 1) * TRK] = placed.astype(BF16)
    head = lax.dot_general(pooled, hold_ref[...], (((0,), (0,)), ((), ())), preferred_element_type=F32)
    for h in range(HEADS):
        for strand in range(2):
            lanes = slice(strand * TRK, (strand + 1) * TRK)
            head_ref[h * DV : h * DV + 128, strand, :] = head[h * 128 : (h + 1) * 128, lanes]
            head_ref[h * DV + 128 : (h + 1) * DV, strand, :] = head[
                512 + h * 64 : 512 + (h + 1) * 64, lanes
            ]


def tail(place, parts, weight, bias, target, strand, sel):
    operands = (*parts, weight, bias, target, strand, sel)
    return pl.pallas_call(
        tail_kernel,
        grid=(1,),
        in_specs=[pl.BlockSpec(memory_space=pltpu.SMEM)]
        + [whole(x.shape) for x in parts]
        + [VMEM] * 5,
        out_specs=(whole((64, TRK)), whole((768, 2, TRK)), whole((2, TRK))),
        out_shape=(
            jax.ShapeDtypeStruct((64, TRK), F32),
            jax.ShapeDtypeStruct((768, 2, TRK), F32),
            jax.ShapeDtypeStruct((2, TRK), F32),
        ),
        scratch_shapes=[
            pltpu.VMEM((512, 768), BF16),
            pltpu.VMEM((512, 768), BF16),
            pltpu.VMEM((768, 768), BF16),
        ],
        compiler_params=pltpu.CompilerParams(vmem_limit_bytes=24 * MIB),
        cost_estimate=pl.CostEstimate(
            flops=4 * 512 * 768 * 768, bytes_accessed=6 * MIB, transcendentals=512 * 384 * 4
        ),
        name="tail",
    )(place, *operands)


def table_kernel(
    place_ref, a_ref, b_ref, c_ref, d_ref, key_ref, sel_key_ref, target_ref, strand_ref, sel_ref,
    chosen_ref, table_ref,
):
    for n, ref in enumerate((a_ref, b_ref, c_ref, d_ref)):
        for j in range(4):
            at = pl.multiple_of(place_ref[n * 4 + j], 96)
            table_ref[pl.ds(at, 96), :] = ref[j * 96 : (j + 1) * 96, :]
    for group in range(16):
        window = group // 8 * 8 + group % 4 * 2 + group // 4 % 2
        rows = slice(group * 32, (group + 1) * 32)
        info = table_ref[window * 96 + 64 : window * 96 + 96, 0:128].astype(F32)
        key = info[:, 0:1] * 16.0 + float(window)
        chosen_ref[rows, :] = jnp.where(key_ref[...] == key, 1.0, 0.0).astype(BF16)
        sel_ref[rows, :] = jnp.where(sel_key_ref[...] == key, 1.0, 0.0).astype(BF16)
        strand_ref[rows, :] = jnp.broadcast_to(info[:, 1:2], (32, 128))
    target_ref[...] = jnp.dot(
        chosen_ref[...], table_ref[...], preferred_element_type=F32
    ).astype(BF16)


def permute(array, axis, target):
    count = lax.axis_size(axis)
    return lax.ppermute(array, axis, [(i, target(i)) for i in range(count)])


def z_up(s):
    return s // 8 * 8 + (s + 1) % 8


def z_down(s):
    return s // 8 * 8 + (s + 7) % 8


def y_over(s):
    return s ^ 8


def join(x, axis, masks):
    return [permute(x, axis, lambda s, m=m: s ^ m) for m in masks]


def stack_kernel(a_ref, b_ref, c_ref, d_ref, out_ref):
    rows = a_ref.shape[0]
    for n, ref in enumerate((a_ref, b_ref, c_ref, d_ref)):
        out_ref[n * rows : (n + 1) * rows, :] = ref[...]


def stacked(parts):
    rows, lanes = parts[0].shape
    return pl.pallas_call(
        stack_kernel,
        in_specs=[VMEM] * 4,
        out_specs=VMEM,
        out_shape=jax.ShapeDtypeStruct((4 * rows, lanes), BF16),
        compiler_params=pltpu.CompilerParams(vmem_limit_bytes=4 * MIB),
        name="stacked",
    )(*parts)


def spread(x):
    near = stacked([x, *join(x, "batch", (2, 4, 6))])
    (over,) = join(near, "batch", (8,))
    return near, over, *join(near, "batch", (1,)), *join(over, "batch", (1,))


def gene_tables(gene_target, gene_owner, gene_strand):
    genes = gene_strand.shape[1]
    owner, strand = gene_owner[0, :, 0], gene_strand[0]
    gene = jnp.arange(genes, dtype=jnp.int32)
    earlier = (owner[:, None] == owner[None, :]) & (gene[None, :] < gene[:, None])
    rank = jnp.sum(earlier.astype(jnp.int32), axis=1)
    lane = jnp.arange(TRK, dtype=jnp.int32)[None]
    slot = (owner * 4 + rank)[:, None]
    info = jnp.where(lane == 0, slot, jnp.where(lane == 1, strand[:, None], 0)).astype(BF16)
    mine = jnp.concatenate([gene_target[0].reshape(64, TRK).astype(BF16), info], axis=0)
    return mine


def gene_rows(place, parts):
    row = jnp.arange(16 * 96, dtype=jnp.int32)
    at = row % 96
    key = jnp.where(at < 64, (row // 96 * 4 + at % 4) * 16 + at // 4, -1)
    lane = jnp.arange(128, dtype=jnp.int32)
    sel_key = jnp.where(lane < 64, (lax.axis_index("batch") * 4 + lane % 4) * 16 + lane // 4, -1)
    operands = (*parts, key.astype(F32)[None], sel_key.astype(F32)[None])
    return pl.pallas_call(
        table_kernel,
        grid=(1,),
        in_specs=[pl.BlockSpec(memory_space=pltpu.SMEM)] + [whole(x.shape) for x in operands],
        out_specs=(whole((512, TRK)), whole((512, 128)), whole((512, 128))),
        out_shape=(
            jax.ShapeDtypeStruct((512, TRK), BF16),
            jax.ShapeDtypeStruct((512, 128), F32),
            jax.ShapeDtypeStruct((512, 128), BF16),
        ),
        scratch_shapes=[pltpu.VMEM((512, 16 * 96), BF16), pltpu.VMEM((16 * 96, TRK), BF16)],
        compiler_params=pltpu.CompilerParams(vmem_limit_bytes=16 * MIB),
        cost_estimate=pl.CostEstimate(
            flops=2 * 512 * 1536 * 384, bytes_accessed=3 * MIB, transcendentals=0
        ),
        name="tables",
    )(place, *operands)


def local(
    tokens,
    filter_tap_weight,
    norm_gain,
    query_weight,
    keyval_weight,
    head_weight,
    head_bias,
    exon_start,
    exon_end,
    gene_strand,
    gene_owner,
    gene_target,
):
    rows = tokens[0]
    row_count = rows.shape[0]
    reach = TAPS // 2 * STRIDE
    tie = lax.optimization_barrier
    bottom, top_rows, mine = tie(
        (rows[row_count - reach :], rows[:reach], gene_tables(gene_target, gene_owner, gene_strand))
    )
    low = lax.ppermute(bottom, "seq", [(i, i + 1) for i in range(15)])
    high = lax.ppermute(top_rows, "seq", [(i + 1, i) for i in range(15)])

    tables = spread(mine)
    low, high, tables = tie((low, high, tables))
    q, own = front(
        rows, low, high, filter_tap_weight, norm_gain[None], query_weight, keyval_weight.T
    )
    me = lax.axis_index("batch")
    y, x, core = me // 8, me // 2 % 4, me % 2
    near = [x, x ^ 1, x ^ 2, x ^ 3]
    spots = [(y, core), (1 - y, core), (y, 1 - core), (1 - y, 1 - core)]
    owner_place = jnp.stack([(b * 8 + a * 2 + c) * 96 for b, c in spots for a in near])
    place = jnp.stack([(b * 2 + c) * 128 for b, c in spots] + [a * 32 for a in near])
    positions = lax.axis_index("seq") * row_count + jnp.arange(row_count, dtype=jnp.int32)
    starts, stops = exon_start[0], exon_end[0]
    inside = (positions >= starts[:, :, None]) & (positions < stops[:, :, None])
    counts = jnp.sum(inside.astype(F32), axis=1).astype(BF16)
    inv_len = 1.0 / jnp.sum((stops - starts).astype(F32), axis=1, keepdims=True)
    weight = head_weight.reshape(HEADS * DV, 2 * TRK)
    bias = head_bias.reshape(1, 2 * TRK)

    def up(x):
        return permute(x, "seq", z_up)

    def down(x):
        return permute(x, "seq", z_down)

    up1, down1 = up(own), down(own)
    over0 = permute(own, "seq", y_over)
    acc, top = attend_first(q, own)
    acc, up1, down1 = tie((acc, up1, down1))
    up2, down2 = up(up1), down(down1)
    over_up1, over_down1 = up(over0), down(over0)
    acc = attend_more(q, top, acc, [up1, down1])
    acc, up2, down2 = tie((acc, up2, down2))
    up3, down3 = up(up2), down(down2)
    acc = attend_more(q, top, acc, [over0, up2, down2])
    acc, over_up1, over_down1 = tie((acc, over_up1, over_down1))
    over_up2, over_down2 = up(over_up1), down(over_down1)
    acc = attend_more(q, top, acc, [over_up1, over_down1])
    acc, up3, down3 = tie((acc, up3, down3))
    up4 = up(up3)
    acc = attend_more(q, top, acc, [up3, down3])
    acc, over_up2, over_down2 = tie((acc, over_up2, over_down2))
    over_up3, over_down3 = up(over_up2), down(over_down2)
    acc = attend_more(q, top, acc, [over_up2, over_down2])
    acc, over_down3 = tie((acc, over_down3))
    over_down4 = down(over_down3)
    acc = attend_more(q, top, acc, [up4, over_down3])
    every = [own, up1, down1, over0, up2, down2, over_up1, over_down1, up3, down3, over_up2,
             over_down2, up4, over_up3, over_down3, over_down4]
    att, pool = attend_last(q, top, acc, counts, inv_len, [over_up3, over_down4], every)

    coverage = coverage_of(att, weight, bias).reshape(1, row_count, 2, TRK)
    target, strand, sel = gene_rows(owner_place.astype(jnp.int32), tables)
    for masks, beside in (((1, 8, 9), coverage), ((2, 4, 6), (target, strand, sel))):
        pieces, beside = tie((join(pool, "seq", masks), beside))
        a, b, c = [piece.astype(F32) for piece in pieces]
        pool = ((pool.astype(F32) + a) + (b + c)).astype(BF16)
        if masks[0] == 1:
            coverage = beside
        else:
            target, strand, sel = beside
    pred, head_grad, bias_grad = tail(
        place.astype(jnp.int32), spread(pool), weight, bias, target, strand, sel
    )
    return (
        coverage,
        pred.reshape(1, 16, 4, TRK),
        head_grad,
        bias_grad,
    )


def solution(mesh):
    in_specs = (
        P("batch", "seq", None),
        P(),
        P(),
        P(),
        P(),
        P(),
        P(),
        P("batch", None, None),
        P("batch", None, None),
        P("batch", None),
        P("batch", None, None),
        P("batch", None, None, None),
    )
    out_specs = (P("batch", "seq", None, None), P("batch", None, None, None), P(), P())
    return jax.shard_map(local, mesh=mesh, in_specs=in_specs, out_specs=out_specs, check_vma=False)
```

```python
import jax
import jax.numpy as jnp
from jax import lax
from jax.experimental import pallas as pl
from jax.experimental.pallas import tpu as pltpu
from jax.sharding import PartitionSpec as P

HEADS = 4
DK = 128
DV = 192
TRK = 384
TAPS = 5
STRIDE = 64
LOG2E = 1.4426950408889634
BIG = 2.0**100
F32 = jnp.float32
BF16 = jnp.bfloat16
MIB = 1024 * 1024
VMEM = pl.BlockSpec(memory_space=pltpu.VMEM)


def whole(shape):
    rank = len(shape)
    return pl.BlockSpec(shape, lambda *grid: (0,) * rank, pipeline_mode=pl.Buffered(1))


def nt_dot(left, right):
    return lax.dot_general(left, right, (((1,), (1,)), ((), ())), preferred_element_type=F32)


def conv_norm(row_blocks, piece, taps_ref, gain_ref, mixed_ref, normed_ref):
    channels = normed_ref.shape[1]
    for n, row_block in enumerate(row_blocks):
        rows = slice(n * STRIDE, (n + 1) * STRIDE)
        squares = jnp.zeros((STRIDE, 128), F32)
        for lane in range(0, channels, 128):
            lanes = slice(lane, lane + 128)
            total = piece(row_block, lanes).astype(F32)
            for k in range(TAPS):
                total = total + taps_ref[k : k + 1, lanes] * piece(
                    row_block + k - TAPS // 2, lanes
                ).astype(F32)
            mixed_ref[rows, lanes] = total
            squares = squares + total * total
        spread = jnp.sum(squares, axis=-1, keepdims=True) / channels
        inverse = lax.rsqrt(spread + 1e-06)
        for lane in range(0, channels, 128):
            lanes = slice(lane, lane + 128)
            normed_ref[rows, lanes] = (mixed_ref[rows, lanes] * inverse * gain_ref[:, lanes]).astype(BF16)


def project(normed_ref, wq_ref, wkv_ref, wide_ref):
    wide_ref[...] = jnp.zeros_like(wide_ref)
    wide_ref[0:64, :] = wkv_ref[256:320, :]
    wide_ref[192:256, :] = wkv_ref[256:320, :]
    queries = jnp.dot(normed_ref[...], wq_ref[...], preferred_element_type=F32)
    queries = (queries * (DK**-0.5 * LOG2E)).astype(BF16)
    first = nt_dot(normed_ref[...], wkv_ref[0:256, :]).astype(BF16)
    rest = nt_dot(normed_ref[...], wide_ref[...]).astype(BF16)
    return queries.astype(F32), first, rest


def inner_kernel(tok_ref, taps_ref, gain_ref, wq_ref, wkv_ref, q_ref, kv_ref, mixed_ref, normed_ref, wide_ref):
    def piece(block, lanes):
        return tok_ref[block * STRIDE : (block + 1) * STRIDE, lanes]

    conv_norm((2, 3, 4, 5), piece, taps_ref, gain_ref, mixed_ref, normed_ref)
    queries, first, rest = project(normed_ref, wq_ref, wkv_ref, wide_ref)
    for h in range(HEADS):
        q_ref[h * 256 : (h + 1) * 256, :] = queries[:, h * DK : (h + 1) * DK]
    kv_ref[0:256, :] = first[:, 0:128]
    kv_ref[256:512, :] = first[:, 128:256]
    kv_ref[512:640, :] = rest[128:256, 128:256]
    kv_ref[640:768, :] = rest[0:128, 0:128]


def edge_kernel(
    tok_ref, low_ref, high_ref, taps_ref, gain_ref, wq_ref, wkv_ref, qi_ref, kvi_ref,
    state_ref, kv_ref, mixed_ref, normed_ref, wide_ref,
):
    def piece(block, lanes):
        if block < 0:
            return low_ref[(block + 2) * STRIDE : (block + 3) * STRIDE, lanes]
        if block >= 8:
            return high_ref[(block - 8) * STRIDE : (block - 7) * STRIDE, lanes]
        return tok_ref[block * STRIDE : (block + 1) * STRIDE, lanes]

    conv_norm((0, 1, 6, 7), piece, taps_ref, gain_ref, mixed_ref, normed_ref)
    queries, first, rest = project(normed_ref, wq_ref, wkv_ref, wide_ref)
    for h in range(HEADS):
        lanes = slice(h * DK, (h + 1) * DK)
        state_ref[h * 512 : h * 512 + 128, 256:384] = queries[0:128, lanes]
        state_ref[h * 512 + 128 : h * 512 + 384, 256:384] = qi_ref[h * 256 : (h + 1) * 256, :]
        state_ref[h * 512 + 384 : h * 512 + 512, 256:384] = queries[128:256, lanes]
    for base, column, source in ((0, 0, 0), (512, 128, 256)):
        kv_ref[base : base + 128, :] = first[0:128, column : column + 128]
        kv_ref[base + 128 : base + 384, :] = kvi_ref[source : source + 256, :]
        kv_ref[base + 384 : base + 512, :] = first[128:256, column : column + 128]
    kv_ref[1024:1152, :] = kvi_ref[512:640, :] + rest[0:128, 0:128]
    kv_ref[1152:1280, :] = kvi_ref[640:768, :] + rest[128:256, 128:256]


def front(tokens, low, high, taps, gain, wq, wkv, extra):
    rows, channels = tokens.shape
    scratch = [pltpu.VMEM((256, channels), F32), pltpu.VMEM((256, channels), BF16)]
    scratch += [pltpu.VMEM((256, channels), BF16)]

    def inner(tokens, taps, gain, wq, wkv):
        return pl.pallas_call(
            inner_kernel,
            out_shape=(
                jax.ShapeDtypeStruct((1024, 128), F32),
                jax.ShapeDtypeStruct((768, 128), BF16),
            ),
            grid=(1,),
            in_specs=[whole(x.shape) for x in (tokens, taps, gain, wq, wkv)],
            out_specs=(VMEM, VMEM),
            scratch_shapes=scratch,
            compiler_params=pltpu.CompilerParams(vmem_limit_bytes=14 * MIB),
            cost_estimate=pl.CostEstimate(
                flops=2 * 256 * channels * 1024, bytes_accessed=5 * MIB, transcendentals=0
            ),
            name="front_inner",
        )(tokens, taps, gain, wq, wkv)

    q_inner, kv_inner = inner(tokens, taps, gain, wq, wkv)
    q_inner, kv_inner, extra = lax.optimization_barrier((q_inner, kv_inner, extra))
    extra = spread(extra)
    operands = (tokens, low, high, taps, gain, wq, wkv, q_inner, kv_inner)
    state, kv = pl.pallas_call(
        edge_kernel,
        grid=(1,),
        in_specs=[whole(x.shape) for x in operands],
        out_specs=(VMEM, VMEM),
        out_shape=(
            jax.ShapeDtypeStruct((2048, 384), F32),
            jax.ShapeDtypeStruct((1280, 128), BF16),
        ),
        scratch_shapes=scratch,
        compiler_params=pltpu.CompilerParams(vmem_limit_bytes=14 * MIB),
        cost_estimate=pl.CostEstimate(
            flops=2 * 256 * channels * 1024, bytes_accessed=6 * MIB, transcendentals=0
        ),
        name="front_edge",
    )(*operands)
    return state, kv, extra


def place_values(kv_ref, base, values_ref, at):
    lane = lax.broadcasted_iota(jnp.int32, (256, 128), 1)
    packed = kv_ref[base + 1024 : base + 1280, :].astype(F32)
    rolled = pltpu.roll(packed, 64, 1)
    one_high = jnp.where(lane == 64, 1.0, 0.0)
    one_low = jnp.where(lane == 0, 1.0, 0.0)
    for parity in range(2):
        values_ref[parity, at : at + 512, 0:128] = kv_ref[base + 512 : base + 1024, :]
    values_ref[0, at : at + 256, 128:256] = jnp.where(lane < 64, packed, one_high).astype(BF16)
    values_ref[0, at + 256 : at + 512, 128:256] = jnp.where(lane < 64, rolled, one_high).astype(BF16)
    values_ref[1, at : at + 256, 128:256] = jnp.where(lane < 64, one_low, rolled).astype(BF16)
    values_ref[1, at + 256 : at + 512, 128:256] = jnp.where(lane < 64, one_low, packed).astype(BF16)


def rows_of(head):
    return pl.ds(pl.multiple_of(head * 512, 512), 512)


def each_pair(body):
    def step(pair, carry):
        for parity in range(2):
            body(pair, parity)
        return carry

    lax.fori_loop(0, HEADS // 2, step, 0)


SPARE = (200, 136)


def queries_of(state_ref, rows):
    return state_ref[rows, 256:384].astype(BF16)


def first_kernel(state_in_ref, kv_ref, state_ref, values_ref):
    place_values(kv_ref, 0, values_ref, 0)
    lane = lax.broadcasted_iota(jnp.int32, (512, 256), 1)

    def one_head(pair, parity):
        rows = rows_of(pair * 2 + parity)
        scores = nt_dot(queries_of(state_in_ref, rows), kv_ref[0:512, :])
        top = jnp.max(scores, axis=1, keepdims=True)
        weights = jnp.exp2(scores - top).astype(BF16)
        acc = jnp.dot(weights, values_ref[parity], preferred_element_type=F32)
        state_ref[rows, 0:256] = jnp.where(lane == SPARE[parity], top, acc)

    each_pair(one_head)


def add_blocks(pair, parity, state_ref, kv_refs, values_ref):
    rows = rows_of(pair * 2 + parity)
    queries, acc = queries_of(state_ref, rows), state_ref[rows, 0:256]
    top = acc[:, SPARE[parity] : SPARE[parity] + 1]
    for n, kv_ref in enumerate(kv_refs):
        scores = nt_dot(queries, kv_ref[0:512, :])
        weights = jnp.exp2(scores - top).astype(BF16)
        acc = acc + jnp.dot(
            weights, values_ref[parity, n * 512 : (n + 1) * 512, :], preferred_element_type=F32
        )
    return acc


def exact_rows(head, part, parity, state_ref, kv_refs, values_ref):
    rows = pl.ds(pl.multiple_of(head * 512 + part * 128, 128), 128)
    queries, acc = queries_of(state_ref, rows), state_ref[rows, 0:256]
    lane = lax.broadcasted_iota(jnp.int32, (128, 256), 1)
    spare = lane == jnp.where(parity == 0, SPARE[0], SPARE[1])
    before = jnp.sum(jnp.where(spare, acc, 0.0), axis=1, keepdims=True)
    scores = [nt_dot(queries, kv_ref[0:512, :]) for kv_ref in kv_refs]
    top = before
    for block in scores:
        top = jnp.maximum(top, jnp.max(block, axis=1, keepdims=True))
    acc = acc * jnp.exp2(before - top)
    for n, block in enumerate(scores):
        weights = jnp.exp2(block - top).astype(BF16)
        acc = acc + jnp.dot(
            weights, values_ref[parity, n * 512 : (n + 1) * 512, :], preferred_element_type=F32
        )
    return rows, jnp.where(spare, top, acc)


def count_outside(outside_ref, acc, parity):
    column = (192, 128)[parity]
    total = acc[:, column : column + 1]
    outside_ref[...] = outside_ref[...] + jnp.where(total < BIG, 0.0, 1.0)
    return total


def more_kernel(state_in_ref, *rest):
    kv_refs, (state_ref, values_ref, outside_ref) = rest[:-3], rest[-3:]
    outside_ref[...] = jnp.zeros_like(outside_ref)
    for n, kv_ref in enumerate(kv_refs):
        place_values(kv_ref, 0, values_ref, n * 512)

    def one_head(pair, parity):
        rows = rows_of(pair * 2 + parity)
        acc = add_blocks(pair, parity, state_in_ref, kv_refs, values_ref)
        state_ref[rows, 0:256] = acc
        state_ref[rows, 256:384] = state_in_ref[rows, 256:384]
        count_outside(outside_ref, acc, parity)

    each_pair(one_head)

    @pl.when(jnp.sum(outside_ref[...]) > 0.0)
    def _():
        def one_part(n, carry):
            head, part = n // 4, lax.rem(n, 4)
            rows, acc = exact_rows(head, part, lax.rem(head, 2), state_in_ref, kv_refs, values_ref)
            state_ref[rows, 0:256] = acc
            return carry

        lax.fori_loop(0, 4 * HEADS, one_part, 0)


def last_kernel(block_count, state_ref, cnt_ref, inv_len_ref, *rest):
    kv_refs, rest = rest[:block_count], rest[block_count:]
    att_ref, pool_ref, values_ref, outside_ref, acc_ref = rest
    lane = lax.broadcasted_iota(jnp.int32, (512, 128), 1)
    outside_ref[...] = jnp.zeros_like(outside_ref)
    for n, kv_ref in enumerate(kv_refs):
        place_values(kv_ref, 0, values_ref, n * 512)

    def finish(pair, accs, totals):
        even, odd = [(acc * (1.0 / total)).astype(BF16) for acc, total in zip(accs, totals)]
        at = [pl.multiple_of(column, 128) for column in (pair * 256, pair * 256 + 128, pair * 128 + 512)]
        att_ref[:, pl.ds(at[0], 128)] = even[:, 0:128]
        att_ref[:, pl.ds(at[1], 128)] = odd[:, 0:128]
        att_ref[:, pl.ds(at[2], 128)] = jnp.where(lane < 64, even[:, 128:256], odd[:, 128:256])

    def one_pair(pair, carry):
        accs = [add_blocks(pair, parity, state_ref, kv_refs, values_ref) for parity in range(2)]
        finish(pair, accs, [count_outside(outside_ref, accs[n], n) for n in range(2)])
        return carry

    lax.fori_loop(0, HEADS // 2, one_pair, 0)

    @pl.when(jnp.sum(outside_ref[...]) > 0.0)
    def _():
        def redo_pair(pair, carry):
            def one_part(n, inner):
                parity, part = n // 4, lax.rem(n, 4)
                rows, acc = exact_rows(pair * 2 + parity, part, parity, state_ref, kv_refs, values_ref)
                acc_ref[parity, pl.ds(pl.multiple_of(part * 128, 128), 128), :] = acc
                return inner

            lax.fori_loop(0, 8, one_part, 0)
            accs = [acc_ref[0], acc_ref[1]]
            finish(pair, accs, [count_outside(outside_ref, accs[n], n) for n in range(2)])
            return carry

        lax.fori_loop(0, HEADS // 2, redo_pair, 0)

    pool = jnp.dot(cnt_ref[...], att_ref[...], preferred_element_type=F32)
    pool_ref[...] = (pool * inv_len_ref[...]).astype(BF16)


def attend_cost(blocks):
    return pl.CostEstimate(
        flops=blocks * 2048 * 512 * 2 * 512,
        bytes_accessed=6 * MIB,
        transcendentals=blocks * 2048 * 512,
    )


STATE = jax.ShapeDtypeStruct((2048, 384), F32)


def attend_first(state, kv):
    return pl.pallas_call(
        first_kernel,
        in_specs=[VMEM, VMEM],
        out_specs=VMEM,
        out_shape=STATE,
        scratch_shapes=[pltpu.VMEM((2, 512, 256), BF16)],
        input_output_aliases={0: 0},
        compiler_params=pltpu.CompilerParams(vmem_limit_bytes=8 * MIB),
        cost_estimate=attend_cost(1),
        name="attend_first",
    )(state, kv)


def attend_more(state, blocks):
    count = len(blocks)
    return pl.pallas_call(
        more_kernel,
        in_specs=[VMEM] * (1 + count),
        out_specs=VMEM,
        out_shape=STATE,
        scratch_shapes=[pltpu.VMEM((2, 512 * count, 256), BF16), pltpu.VMEM((512, 1), F32)],
        compiler_params=pltpu.CompilerParams(vmem_limit_bytes=8 * MIB),
        cost_estimate=attend_cost(count),
        name="attend_more",
    )(state, *blocks)


def attend_last(state, counts, inv_len, blocks):
    count = len(blocks)

    def kernel(*refs):
        last_kernel(count, *refs)

    return pl.pallas_call(
        kernel,
        in_specs=[VMEM] * (3 + count),
        out_specs=(VMEM, VMEM),
        out_shape=(jax.ShapeDtypeStruct((512, 768), BF16), jax.ShapeDtypeStruct((32, 768), BF16)),
        scratch_shapes=[
            pltpu.VMEM((2, 512 * count, 256), BF16),
            pltpu.VMEM((512, 1), F32),
            pltpu.VMEM((2, 512, 256), F32),
        ],
        compiler_params=pltpu.CompilerParams(vmem_limit_bytes=8 * MIB),
        cost_estimate=attend_cost(count),
        name="attend_last",
    )(state, counts, inv_len, *blocks)


def soft_plus(x):
    return jnp.maximum(x, 0.0) + jnp.log1p(jnp.exp(-jnp.abs(x)))


def order_rows(weight_ref, ordered_ref):
    for h in range(HEADS):
        ordered_ref[h * 128 : (h + 1) * 128, :] = weight_ref[h * DV : h * DV + 128, :]
        ordered_ref[512 + h * 64 : 512 + (h + 1) * 64, :] = weight_ref[h * DV + 128 : (h + 1) * DV, :]


def coverage_kernel(att_ref, weight_ref, bias_ref, out_ref, ordered_ref):
    order_rows(weight_ref, ordered_ref)

    def step(n, carry):
        rows = pl.ds(pl.multiple_of(n * 128, 128), 128)
        logits = jnp.dot(att_ref[rows, :], ordered_ref[...], preferred_element_type=F32)
        out_ref[rows, :] = soft_plus(logits + bias_ref[...]).astype(BF16)
        return carry

    lax.fori_loop(0, 4, step, 0)


def coverage_of(att, weight, bias):
    return pl.pallas_call(
        coverage_kernel,
        in_specs=[VMEM] * 3,
        out_specs=VMEM,
        out_shape=jax.ShapeDtypeStruct((512, 768), BF16),
        scratch_shapes=[pltpu.VMEM((768, 768), BF16)],
        compiler_params=pltpu.CompilerParams(vmem_limit_bytes=8 * MIB),
        cost_estimate=pl.CostEstimate(
            flops=2 * 512 * 768 * 768, bytes_accessed=3 * MIB, transcendentals=512 * 768 * 2
        ),
        name="coverage",
    )(att, weight, bias)


def tail_kernel(
    place_ref, a_ref, b_ref, weight_ref, bias_ref, target_ref, strand_ref, sel_ref,
    pred_ref, head_ref, bias_grad_ref, pooled_ref, hold_ref, ordered_ref,
):
    order_rows(weight_ref, ordered_ref)
    for n, ref in enumerate((a_ref, b_ref)):
        for j in range(8):
            at = pl.multiple_of(place_ref[n * 8 + j], 32)
            pooled_ref[pl.ds(at, 32), :] = ref[j * 32 : (j + 1) * 32, :]
    pooled = pooled_ref[...]
    logits = jnp.dot(pooled, ordered_ref[...], preferred_element_type=F32) + bias_ref[...]
    plus = strand_ref[:, 0:1] < 0.5
    logit = jnp.where(plus, logits[:, 0:TRK], logits[:, TRK : 2 * TRK])
    decay = jnp.exp(-jnp.abs(logit))
    pred = jnp.maximum(logit, 0.0) + jnp.log1p(decay)
    slope = (jnp.log1p(pred) - target_ref[...].astype(F32)) / (1.0 + pred)
    grad = slope * (jnp.where(logit >= 0.0, 1.0, decay) / (1.0 + decay))
    pred_ref[...] = lax.dot_general(
        sel_ref[...], pred.astype(BF16), (((0,), (0,)), ((), ())), preferred_element_type=F32
    )[0:64]
    for strand in range(2):
        placed = jnp.where(plus == (strand == 0), grad, 0.0)
        bias_grad_ref[strand : strand + 1, :] = jnp.sum(placed, axis=0, keepdims=True)
        hold_ref[:, strand * TRK : (strand + 1) * TRK] = placed.astype(BF16)
    head = lax.dot_general(pooled, hold_ref[...], (((0,), (0,)), ((), ())), preferred_element_type=F32)
    for h in range(HEADS):
        for strand in range(2):
            lanes = slice(strand * TRK, (strand + 1) * TRK)
            head_ref[h * DV : h * DV + 128, strand, :] = head[h * 128 : (h + 1) * 128, lanes]
            head_ref[h * DV + 128 : (h + 1) * DV, strand, :] = head[
                512 + h * 64 : 512 + (h + 1) * 64, lanes
            ]


def tail(place, parts, weight, bias, target, strand, sel):
    operands = (*parts, weight, bias, target, strand, sel)
    return pl.pallas_call(
        tail_kernel,
        grid=(1,),
        in_specs=[pl.BlockSpec(memory_space=pltpu.SMEM)]
        + [whole(x.shape) for x in parts]
        + [VMEM] * 5,
        out_specs=(whole((64, TRK)), whole((768, 2, TRK)), whole((2, TRK))),
        out_shape=(
            jax.ShapeDtypeStruct((64, TRK), F32),
            jax.ShapeDtypeStruct((768, 2, TRK), F32),
            jax.ShapeDtypeStruct((2, TRK), F32),
        ),
        scratch_shapes=[
            pltpu.VMEM((512, 768), BF16),
            pltpu.VMEM((512, 768), BF16),
            pltpu.VMEM((768, 768), BF16),
        ],
        compiler_params=pltpu.CompilerParams(vmem_limit_bytes=24 * MIB),
        cost_estimate=pl.CostEstimate(
            flops=4 * 512 * 768 * 768, bytes_accessed=6 * MIB, transcendentals=512 * 384 * 4
        ),
        name="tail",
    )(place, *operands)


def table_kernel(
    place_ref, a_ref, b_ref, key_ref, sel_key_ref, target_ref, strand_ref, sel_ref,
    chosen_ref, table_ref,
):
    for n, ref in enumerate((a_ref, b_ref)):
        for j in range(8):
            at = pl.multiple_of(place_ref[n * 8 + j], 96)
            table_ref[pl.ds(at, 96), :] = ref[j * 96 : (j + 1) * 96, :]
    for group in range(16):
        window = group // 8 * 8 + group % 4 * 2 + group // 4 % 2
        rows = slice(group * 32, (group + 1) * 32)
        info = table_ref[window * 96 + 64 : window * 96 + 96, 0:128].astype(F32)
        key = info[:, 0:1] * 16.0 + float(window)
        chosen_ref[rows, :] = jnp.where(key_ref[...] == key, 1.0, 0.0).astype(BF16)
        sel_ref[rows, :] = jnp.where(sel_key_ref[...] == key, 1.0, 0.0).astype(BF16)
        strand_ref[rows, :] = jnp.broadcast_to(info[:, 1:2], (32, 128))
    target_ref[...] = jnp.dot(
        chosen_ref[...], table_ref[...], preferred_element_type=F32
    ).astype(BF16)


def permute(array, axis, target):
    count = lax.axis_size(axis)
    return lax.ppermute(array, axis, [(i, target(i)) for i in range(count)])


def z_up(s):
    return s // 8 * 8 + (s + 1) % 8


def z_down(s):
    return s // 8 * 8 + (s + 7) % 8


def y_over(s):
    return s ^ 8


def join(x, axis, masks):
    return [permute(x, axis, lambda s, m=m: s ^ m) for m in masks]


def stack_kernel(*refs):
    parts, out_ref = refs[:-1], refs[-1]
    rows = parts[0].shape[0]
    for n, ref in enumerate(parts):
        out_ref[n * rows : (n + 1) * rows, :] = ref[...]


def stacked(parts):
    rows, lanes = parts[0].shape
    return pl.pallas_call(
        stack_kernel,
        in_specs=[VMEM] * len(parts),
        out_specs=VMEM,
        out_shape=jax.ShapeDtypeStruct((len(parts) * rows, lanes), BF16),
        compiler_params=pltpu.CompilerParams(vmem_limit_bytes=4 * MIB),
        name="stacked",
    )(*parts)


def spread(x):
    both = stacked([x, *join(x, "batch", (8,))])
    near = stacked([both, *join(both, "batch", (2, 4, 6))])
    return near, *join(near, "batch", (1,))


def gene_tables(gene_target, gene_owner, gene_strand):
    genes = gene_strand.shape[1]
    owner, strand = gene_owner[0, :, 0], gene_strand[0]
    gene = jnp.arange(genes, dtype=jnp.int32)
    earlier = (owner[:, None] == owner[None, :]) & (gene[None, :] < gene[:, None])
    rank = jnp.sum(earlier.astype(jnp.int32), axis=1)
    lane = jnp.arange(TRK, dtype=jnp.int32)[None]
    slot = (owner * 4 + rank)[:, None]
    info = jnp.where(lane == 0, slot, jnp.where(lane == 1, strand[:, None], 0)).astype(BF16)
    mine = jnp.concatenate([gene_target[0].reshape(64, TRK).astype(BF16), info], axis=0)
    return mine


def gene_rows(place, parts):
    row = jnp.arange(16 * 96, dtype=jnp.int32)
    at = row % 96
    key = jnp.where(at < 64, (row // 96 * 4 + at % 4) * 16 + at // 4, -1)
    lane = jnp.arange(128, dtype=jnp.int32)
    sel_key = jnp.where(lane < 64, (lax.axis_index("batch") * 4 + lane % 4) * 16 + lane // 4, -1)
    operands = (*parts, key.astype(F32)[None], sel_key.astype(F32)[None])
    return pl.pallas_call(
        table_kernel,
        grid=(1,),
        in_specs=[pl.BlockSpec(memory_space=pltpu.SMEM)] + [whole(x.shape) for x in operands],
        out_specs=(whole((512, TRK)), whole((512, 128)), whole((512, 128))),
        out_shape=(
            jax.ShapeDtypeStruct((512, TRK), BF16),
            jax.ShapeDtypeStruct((512, 128), F32),
            jax.ShapeDtypeStruct((512, 128), BF16),
        ),
        scratch_shapes=[pltpu.VMEM((512, 16 * 96), BF16), pltpu.VMEM((16 * 96, TRK), BF16)],
        compiler_params=pltpu.CompilerParams(vmem_limit_bytes=16 * MIB),
        cost_estimate=pl.CostEstimate(
            flops=2 * 512 * 1536 * 384, bytes_accessed=3 * MIB, transcendentals=0
        ),
        name="tables",
    )(place, *operands)


def local(
    tokens,
    filter_tap_weight,
    norm_gain,
    query_weight,
    keyval_weight,
    head_weight,
    head_bias,
    exon_start,
    exon_end,
    gene_strand,
    gene_owner,
    gene_target,
):
    rows = tokens[0]
    row_count = rows.shape[0]
    reach = TAPS // 2 * STRIDE
    tie = lax.optimization_barrier
    low = lax.ppermute(rows[row_count - reach :], "seq", [(i, i + 1) for i in range(15)])
    high = lax.ppermute(rows[:reach], "seq", [(i + 1, i) for i in range(15)])

    acc, own, tables = front(
        rows, low, high, filter_tap_weight, norm_gain[None], query_weight, keyval_weight.T,
        gene_tables(gene_target, gene_owner, gene_strand),
    )
    me = lax.axis_index("batch")
    y, x, core = me // 8, me // 2 % 4, me % 2
    near = [x, x ^ 1, x ^ 2, x ^ 3]
    spots = [(b, a, c) for c in (core, 1 - core) for a in near for b in (y, 1 - y)]
    owner_place = jnp.stack([(b * 8 + a * 2 + c) * 96 for b, a, c in spots]).astype(jnp.int32)
    place = jnp.stack([((b * 2 + c) * 4 + a) * 32 for b, a, c in spots]).astype(jnp.int32)
    positions = lax.axis_index("seq") * row_count + jnp.arange(row_count, dtype=jnp.int32)
    starts, stops = exon_start[0], exon_end[0]
    inside = (positions >= starts[:, :, None]) & (positions < stops[:, :, None])
    counts = jnp.sum(inside.astype(F32), axis=1).astype(BF16)
    inv_len = 1.0 / jnp.sum((stops - starts).astype(F32), axis=1, keepdims=True)
    weight = head_weight.reshape(HEADS * DV, 2 * TRK)
    bias = head_bias.reshape(1, 2 * TRK)

    def up(x):
        return permute(x, "seq", z_up)

    def down(x):
        return permute(x, "seq", z_down)

    up1, down1 = up(own), down(own)
    over0 = permute(own, "seq", y_over)
    acc = attend_first(acc, own)
    acc, up1, down1 = tie((acc, up1, down1))
    up2, down2 = up(up1), down(down1)
    over_up1, over_down1 = up(over0), down(over0)
    acc = attend_more(acc, [up1, down1])
    acc, up2, down2 = tie((acc, up2, down2))
    up3, down3 = up(up2), down(down2)
    acc = attend_more(acc, [over0, up2, down2])
    acc, over_up1, over_down1 = tie((acc, over_up1, over_down1))
    over_up2, over_down2 = up(over_up1), down(over_down1)
    acc = attend_more(acc, [over_up1, over_down1])
    acc, up3, down3 = tie((acc, up3, down3))
    up4 = up(up3)
    acc = attend_more(acc, [up3, down3])
    acc, over_up2, over_down2 = tie((acc, over_up2, over_down2))
    over_up3, over_down3 = up(over_up2), down(over_down2)
    acc = attend_more(acc, [over_up2, over_down2])
    target, strand, sel = gene_rows(owner_place, tables)
    acc, over_down3, target, strand, sel = tie((acc, over_down3, target, strand, sel))
    over_down4 = down(over_down3)
    acc = attend_more(acc, [up4, over_down3])
    att, pool = attend_last(acc, counts, inv_len, [over_up3, over_down4])

    coverage = coverage_of(att, weight, bias).reshape(1, row_count, 2, TRK)
    for masks in ((1, 8, 9), (2, 4, 6)):
        pieces, coverage = tie((join(pool, "seq", masks), coverage))
        a, b, c = [piece.astype(F32) for piece in pieces]
        pool = ((pool.astype(F32) + a) + (b + c)).astype(BF16)
    pred, head_grad, bias_grad = tail(
        place, spread(pool), weight, bias, target, strand, sel
    )
    return (
        coverage,
        pred.reshape(1, 16, 4, TRK),
        head_grad,
        bias_grad,
    )


def solution(mesh):
    in_specs = (
        P("batch", "seq", None),
        P(),
        P(),
        P(),
        P(),
        P(),
        P(),
        P("batch", None, None),
        P("batch", None, None),
        P("batch", None),
        P("batch", None, None),
        P("batch", None, None, None),
    )
    out_specs = (P("batch", "seq", None, None), P("batch", None, None, None), P(), P())
    return jax.shard_map(local, mesh=mesh, in_specs=in_specs, out_specs=out_specs, check_vma=False)
```

```python
import jax
import jax.numpy as jnp
from jax import lax
from jax.experimental import pallas as pl
from jax.experimental.pallas import tpu as pltpu
from jax.sharding import PartitionSpec as P

HEADS = 4
DK = 128
DV = 192
TRK = 384
TAPS = 5
STRIDE = 64
LOG2E = 1.4426950408889634
BIG = 2.0**100
F32 = jnp.float32
BF16 = jnp.bfloat16
MIB = 1024 * 1024
VMEM = pl.BlockSpec(memory_space=pltpu.VMEM)


def whole(shape):
    rank = len(shape)
    return pl.BlockSpec(shape, lambda *grid: (0,) * rank, pipeline_mode=pl.Buffered(1))


def nt_dot(left, right):
    return lax.dot_general(left, right, (((1,), (1,)), ((), ())), preferred_element_type=F32)


def conv_norm(row_blocks, piece, taps_ref, gain_ref, mixed_ref, normed_ref):
    channels = normed_ref.shape[1]
    for n, row_block in enumerate(row_blocks):
        rows = slice(n * STRIDE, (n + 1) * STRIDE)
        squares = jnp.zeros((STRIDE, 128), F32)
        for lane in range(0, channels, 128):
            lanes = slice(lane, lane + 128)
            total = piece(row_block, lanes).astype(F32)
            for k in range(TAPS):
                total = total + taps_ref[k : k + 1, lanes] * piece(
                    row_block + k - TAPS // 2, lanes
                ).astype(F32)
            mixed_ref[rows, lanes] = total
            squares = squares + total * total
        spread = jnp.sum(squares, axis=-1, keepdims=True) / channels
        inverse = lax.rsqrt(spread + 1e-06)
        for lane in range(0, channels, 128):
            lanes = slice(lane, lane + 128)
            normed_ref[rows, lanes] = (mixed_ref[rows, lanes] * inverse * gain_ref[:, lanes]).astype(BF16)


def project(normed_ref, wq_ref, wkv_ref, wide_ref):
    wide_ref[...] = jnp.zeros_like(wide_ref)
    wide_ref[0:64, :] = wkv_ref[256:320, :]
    wide_ref[192:256, :] = wkv_ref[256:320, :]
    queries = jnp.dot(normed_ref[...], wq_ref[...], preferred_element_type=F32)
    queries = (queries * (DK**-0.5 * LOG2E)).astype(BF16)
    first = nt_dot(normed_ref[...], wkv_ref[0:256, :]).astype(BF16)
    rest = nt_dot(normed_ref[...], wide_ref[...]).astype(BF16)
    return queries.astype(F32), first, rest


def inner_kernel(tok_ref, taps_ref, gain_ref, wq_ref, wkv_ref, q_ref, kv_ref, mixed_ref, normed_ref, wide_ref):
    def piece(block, lanes):
        return tok_ref[block * STRIDE : (block + 1) * STRIDE, lanes]

    conv_norm((2, 3, 4, 5), piece, taps_ref, gain_ref, mixed_ref, normed_ref)
    queries, first, rest = project(normed_ref, wq_ref, wkv_ref, wide_ref)
    for h in range(HEADS):
        q_ref[h * 256 : (h + 1) * 256, :] = queries[:, h * DK : (h + 1) * DK]
    kv_ref[0:256, :] = first[:, 0:128]
    kv_ref[256:512, :] = first[:, 128:256]
    kv_ref[512:640, :] = rest[128:256, 128:256]
    kv_ref[640:768, :] = rest[0:128, 0:128]


def edge_kernel(
    tok_ref, low_ref, high_ref, taps_ref, gain_ref, wq_ref, wkv_ref, qi_ref, kvi_ref,
    state_ref, kv_ref, mixed_ref, normed_ref, wide_ref,
):
    def piece(block, lanes):
        if block < 0:
            return low_ref[(block + 2) * STRIDE : (block + 3) * STRIDE, lanes]
        if block >= 8:
            return high_ref[(block - 8) * STRIDE : (block - 7) * STRIDE, lanes]
        return tok_ref[block * STRIDE : (block + 1) * STRIDE, lanes]

    conv_norm((0, 1, 6, 7), piece, taps_ref, gain_ref, mixed_ref, normed_ref)
    queries, first, rest = project(normed_ref, wq_ref, wkv_ref, wide_ref)
    for h in range(HEADS):
        lanes = slice(h * DK, (h + 1) * DK)
        state_ref[h * 512 : h * 512 + 128, 256:384] = queries[0:128, lanes]
        state_ref[h * 512 + 128 : h * 512 + 384, 256:384] = qi_ref[h * 256 : (h + 1) * 256, :]
        state_ref[h * 512 + 384 : h * 512 + 512, 256:384] = queries[128:256, lanes]
    for base, column, source in ((0, 0, 0), (512, 128, 256)):
        kv_ref[base : base + 128, :] = first[0:128, column : column + 128]
        kv_ref[base + 128 : base + 384, :] = kvi_ref[source : source + 256, :]
        kv_ref[base + 384 : base + 512, :] = first[128:256, column : column + 128]
    kv_ref[1024:1152, :] = kvi_ref[512:640, :] + rest[0:128, 0:128]
    kv_ref[1152:1280, :] = kvi_ref[640:768, :] + rest[128:256, 128:256]


def front(tokens, low, high, taps, gain, wq, wkv, extra):
    rows, channels = tokens.shape
    scratch = [pltpu.VMEM((256, channels), F32), pltpu.VMEM((256, channels), BF16)]
    scratch += [pltpu.VMEM((256, channels), BF16)]

    def inner(tokens, taps, gain, wq, wkv):
        return pl.pallas_call(
            inner_kernel,
            out_shape=(
                jax.ShapeDtypeStruct((1024, 128), F32),
                jax.ShapeDtypeStruct((768, 128), BF16),
            ),
            grid=(1,),
            in_specs=[whole(x.shape) for x in (tokens, taps, gain, wq, wkv)],
            out_specs=(VMEM, VMEM),
            scratch_shapes=scratch,
            compiler_params=pltpu.CompilerParams(vmem_limit_bytes=14 * MIB),
            cost_estimate=pl.CostEstimate(
                flops=2 * 256 * channels * 1024, bytes_accessed=5 * MIB, transcendentals=0
            ),
            name="front_inner",
        )(tokens, taps, gain, wq, wkv)

    q_inner, kv_inner = inner(tokens, taps, gain, wq, wkv)
    q_inner, kv_inner, extra = lax.optimization_barrier((q_inner, kv_inner, extra))
    extra = across(extra)
    operands = (tokens, low, high, taps, gain, wq, wkv, q_inner, kv_inner)
    state, kv = pl.pallas_call(
        edge_kernel,
        grid=(1,),
        in_specs=[whole(x.shape) for x in operands],
        out_specs=(VMEM, VMEM),
        out_shape=(
            jax.ShapeDtypeStruct((2048, 384), F32),
            jax.ShapeDtypeStruct((1280, 128), BF16),
        ),
        scratch_shapes=scratch,
        compiler_params=pltpu.CompilerParams(vmem_limit_bytes=14 * MIB),
        cost_estimate=pl.CostEstimate(
            flops=2 * 256 * channels * 1024, bytes_accessed=6 * MIB, transcendentals=0
        ),
        name="front_edge",
    )(*operands)
    return state, kv, extra


def place_values(kv_ref, base, values_ref, at):
    lane = lax.broadcasted_iota(jnp.int32, (256, 128), 1)
    packed = kv_ref[base + 1024 : base + 1280, :].astype(F32)
    rolled = pltpu.roll(packed, 64, 1)
    one_high = jnp.where(lane == 64, 1.0, 0.0)
    one_low = jnp.where(lane == 0, 1.0, 0.0)
    for parity in range(2):
        values_ref[parity, at : at + 512, 0:128] = kv_ref[base + 512 : base + 1024, :]
    values_ref[0, at : at + 256, 128:256] = jnp.where(lane < 64, packed, one_high).astype(BF16)
    values_ref[0, at + 256 : at + 512, 128:256] = jnp.where(lane < 64, rolled, one_high).astype(BF16)
    values_ref[1, at : at + 256, 128:256] = jnp.where(lane < 64, one_low, rolled).astype(BF16)
    values_ref[1, at + 256 : at + 512, 128:256] = jnp.where(lane < 64, one_low, packed).astype(BF16)


def rows_of(head):
    return pl.ds(pl.multiple_of(head * 512, 512), 512)


def each_pair(body):
    def step(pair, carry):
        for parity in range(2):
            body(pair, parity)
        return carry

    lax.fori_loop(0, HEADS // 2, step, 0)


SPARE = (200, 136)


def queries_of(state_ref, rows):
    return state_ref[rows, 256:384].astype(BF16)


def first_kernel(state_in_ref, kv_ref, state_ref, values_ref):
    place_values(kv_ref, 0, values_ref, 0)
    lane = lax.broadcasted_iota(jnp.int32, (512, 256), 1)

    def one_head(pair, parity):
        rows = rows_of(pair * 2 + parity)
        scores = nt_dot(queries_of(state_in_ref, rows), kv_ref[0:512, :])
        top = jnp.max(scores, axis=1, keepdims=True)
        weights = jnp.exp2(scores - top).astype(BF16)
        acc = jnp.dot(weights, values_ref[parity], preferred_element_type=F32)
        state_ref[rows, 0:256] = jnp.where(lane == SPARE[parity], top, acc)

    each_pair(one_head)


def add_blocks(pair, parity, state_ref, kv_refs, values_ref):
    rows = rows_of(pair * 2 + parity)
    queries, acc = queries_of(state_ref, rows), state_ref[rows, 0:256]
    top = acc[:, SPARE[parity] : SPARE[parity] + 1]
    for n, kv_ref in enumerate(kv_refs):
        scores = nt_dot(queries, kv_ref[0:512, :])
        weights = jnp.exp2(scores - top).astype(BF16)
        acc = acc + jnp.dot(
            weights, values_ref[parity, n * 512 : (n + 1) * 512, :], preferred_element_type=F32
        )
    return acc


def exact_rows(head, part, parity, state_ref, kv_refs, values_ref):
    rows = pl.ds(pl.multiple_of(head * 512 + part * 128, 128), 128)
    queries, acc = queries_of(state_ref, rows), state_ref[rows, 0:256]
    lane = lax.broadcasted_iota(jnp.int32, (128, 256), 1)
    spare = lane == jnp.where(parity == 0, SPARE[0], SPARE[1])
    before = jnp.sum(jnp.where(spare, acc, 0.0), axis=1, keepdims=True)
    scores = [nt_dot(queries, kv_ref[0:512, :]) for kv_ref in kv_refs]
    top = before
    for block in scores:
        top = jnp.maximum(top, jnp.max(block, axis=1, keepdims=True))
    acc = acc * jnp.exp2(before - top)
    for n, block in enumerate(scores):
        weights = jnp.exp2(block - top).astype(BF16)
        acc = acc + jnp.dot(
            weights, values_ref[parity, n * 512 : (n + 1) * 512, :], preferred_element_type=F32
        )
    return rows, jnp.where(spare, top, acc)


def count_outside(outside_ref, acc, parity):
    column = (192, 128)[parity]
    total = acc[:, column : column + 1]
    outside_ref[...] = outside_ref[...] + jnp.where(total < BIG, 0.0, 1.0)
    return total


def more_kernel(state_in_ref, *rest):
    kv_refs, (state_ref, values_ref, outside_ref) = rest[:-3], rest[-3:]
    outside_ref[...] = jnp.zeros_like(outside_ref)
    for n, kv_ref in enumerate(kv_refs):
        place_values(kv_ref, 0, values_ref, n * 512)

    def one_head(pair, parity):
        rows = rows_of(pair * 2 + parity)
        acc = add_blocks(pair, parity, state_in_ref, kv_refs, values_ref)
        state_ref[rows, 0:256] = acc
        state_ref[rows, 256:384] = state_in_ref[rows, 256:384]
        count_outside(outside_ref, acc, parity)

    each_pair(one_head)

    @pl.when(jnp.sum(outside_ref[...]) > 0.0)
    def _():
        def one_part(n, carry):
            head, part = n // 4, lax.rem(n, 4)
            rows, acc = exact_rows(head, part, lax.rem(head, 2), state_in_ref, kv_refs, values_ref)
            state_ref[rows, 0:256] = acc
            return carry

        lax.fori_loop(0, 4 * HEADS, one_part, 0)


def last_kernel(block_count, state_ref, cnt_ref, inv_len_ref, *rest):
    kv_refs, rest = rest[:block_count], rest[block_count:]
    att_ref, pool_ref, values_ref, outside_ref, acc_ref = rest
    lane = lax.broadcasted_iota(jnp.int32, (512, 128), 1)
    outside_ref[...] = jnp.zeros_like(outside_ref)
    for n, kv_ref in enumerate(kv_refs):
        place_values(kv_ref, 0, values_ref, n * 512)

    def finish(pair, accs, totals):
        even, odd = [(acc * (1.0 / total)).astype(BF16) for acc, total in zip(accs, totals)]
        at = [pl.multiple_of(column, 128) for column in (pair * 256, pair * 256 + 128, pair * 128 + 512)]
        att_ref[:, pl.ds(at[0], 128)] = even[:, 0:128]
        att_ref[:, pl.ds(at[1], 128)] = odd[:, 0:128]
        att_ref[:, pl.ds(at[2], 128)] = jnp.where(lane < 64, even[:, 128:256], odd[:, 128:256])

    def one_pair(pair, carry):
        accs = [add_blocks(pair, parity, state_ref, kv_refs, values_ref) for parity in range(2)]
        finish(pair, accs, [count_outside(outside_ref, accs[n], n) for n in range(2)])
        return carry

    lax.fori_loop(0, HEADS // 2, one_pair, 0)

    @pl.when(jnp.sum(outside_ref[...]) > 0.0)
    def _():
        def redo_pair(pair, carry):
            def one_part(n, inner):
                parity, part = n // 4, lax.rem(n, 4)
                rows, acc = exact_rows(pair * 2 + parity, part, parity, state_ref, kv_refs, values_ref)
                acc_ref[parity, pl.ds(pl.multiple_of(part * 128, 128), 128), :] = acc
                return inner

            lax.fori_loop(0, 8, one_part, 0)
            accs = [acc_ref[0], acc_ref[1]]
            finish(pair, accs, [count_outside(outside_ref, accs[n], n) for n in range(2)])
            return carry

        lax.fori_loop(0, HEADS // 2, redo_pair, 0)

    pool = jnp.dot(cnt_ref[...], att_ref[...], preferred_element_type=F32)
    pool_ref[...] = (pool * inv_len_ref[...]).astype(BF16)


def attend_cost(blocks):
    return pl.CostEstimate(
        flops=blocks * 2048 * 512 * 2 * 512,
        bytes_accessed=6 * MIB,
        transcendentals=blocks * 2048 * 512,
    )


STATE = jax.ShapeDtypeStruct((2048, 384), F32)


def attend_first(state, kv):
    return pl.pallas_call(
        first_kernel,
        in_specs=[VMEM, VMEM],
        out_specs=VMEM,
        out_shape=STATE,
        scratch_shapes=[pltpu.VMEM((2, 512, 256), BF16)],
        input_output_aliases={0: 0},
        compiler_params=pltpu.CompilerParams(vmem_limit_bytes=8 * MIB),
        cost_estimate=attend_cost(1),
        name="attend_first",
    )(state, kv)


def attend_more(state, blocks):
    count = len(blocks)
    return pl.pallas_call(
        more_kernel,
        in_specs=[VMEM] * (1 + count),
        out_specs=VMEM,
        out_shape=STATE,
        scratch_shapes=[pltpu.VMEM((2, 512 * count, 256), BF16), pltpu.VMEM((512, 1), F32)],
        compiler_params=pltpu.CompilerParams(vmem_limit_bytes=8 * MIB),
        cost_estimate=attend_cost(count),
        name="attend_more",
    )(state, *blocks)


def attend_last(state, counts, inv_len, blocks):
    count = len(blocks)

    def kernel(*refs):
        last_kernel(count, *refs)

    return pl.pallas_call(
        kernel,
        in_specs=[VMEM] * (3 + count),
        out_specs=(VMEM, VMEM),
        out_shape=(jax.ShapeDtypeStruct((512, 768), BF16), jax.ShapeDtypeStruct((32, 768), BF16)),
        scratch_shapes=[
            pltpu.VMEM((2, 512 * count, 256), BF16),
            pltpu.VMEM((512, 1), F32),
            pltpu.VMEM((2, 512, 256), F32),
        ],
        compiler_params=pltpu.CompilerParams(vmem_limit_bytes=8 * MIB),
        cost_estimate=attend_cost(count),
        name="attend_last",
    )(state, counts, inv_len, *blocks)


def soft_plus(x):
    return jnp.maximum(x, 0.0) + jnp.log1p(jnp.exp(-jnp.abs(x)))


def order_rows(weight_ref, ordered_ref):
    for h in range(HEADS):
        ordered_ref[h * 128 : (h + 1) * 128, :] = weight_ref[h * DV : h * DV + 128, :]
        ordered_ref[512 + h * 64 : 512 + (h + 1) * 64, :] = weight_ref[h * DV + 128 : (h + 1) * DV, :]


def coverage_kernel(att_ref, weight_ref, bias_ref, out_ref, ordered_ref):
    order_rows(weight_ref, ordered_ref)

    def step(n, carry):
        rows = pl.ds(pl.multiple_of(n * 128, 128), 128)
        logits = jnp.dot(att_ref[rows, :], ordered_ref[...], preferred_element_type=F32)
        out_ref[rows, :] = soft_plus(logits + bias_ref[...]).astype(BF16)
        return carry

    lax.fori_loop(0, 4, step, 0)


def coverage_of(att, weight, bias):
    return pl.pallas_call(
        coverage_kernel,
        in_specs=[VMEM] * 3,
        out_specs=VMEM,
        out_shape=jax.ShapeDtypeStruct((512, 768), BF16),
        scratch_shapes=[pltpu.VMEM((768, 768), BF16)],
        compiler_params=pltpu.CompilerParams(vmem_limit_bytes=8 * MIB),
        cost_estimate=pl.CostEstimate(
            flops=2 * 512 * 768 * 768, bytes_accessed=3 * MIB, transcendentals=512 * 768 * 2
        ),
        name="coverage",
    )(att, weight, bias)


def tail_kernel(
    place_ref, a_ref, b_ref, weight_ref, bias_ref, target_ref, strand_ref, sel_ref,
    pred_ref, head_ref, bias_grad_ref, pooled_ref, hold_ref, ordered_ref,
):
    order_rows(weight_ref, ordered_ref)
    for n, ref in enumerate((a_ref, b_ref)):
        for j in range(8):
            at = pl.multiple_of(place_ref[n * 8 + j], 32)
            pooled_ref[pl.ds(at, 32), :] = ref[j * 32 : (j + 1) * 32, :]
    pooled = pooled_ref[...]
    logits = jnp.dot(pooled, ordered_ref[...], preferred_element_type=F32) + bias_ref[...]
    plus = strand_ref[:, 0:1] < 0.5
    logit = jnp.where(plus, logits[:, 0:TRK], logits[:, TRK : 2 * TRK])
    decay = jnp.exp(-jnp.abs(logit))
    pred = jnp.maximum(logit, 0.0) + jnp.log1p(decay)
    slope = (jnp.log1p(pred) - target_ref[...].astype(F32)) / (1.0 + pred)
    grad = slope * (jnp.where(logit >= 0.0, 1.0, decay) / (1.0 + decay))
    chosen = lax.dot_general(
        sel_ref[...], pred.astype(BF16), (((0,), (0,)), ((), ())), preferred_element_type=F32
    )
    for window in range(16):
        pred_ref[window] = chosen[window * 4 : window * 4 + 4]
    for strand in range(2):
        placed = jnp.where(plus == (strand == 0), grad, 0.0)
        bias_grad_ref[strand : strand + 1, :] = jnp.sum(placed, axis=0, keepdims=True)
        hold_ref[:, strand * TRK : (strand + 1) * TRK] = placed.astype(BF16)
    head = lax.dot_general(pooled, hold_ref[...], (((0,), (0,)), ((), ())), preferred_element_type=F32)
    for h in range(HEADS):
        for strand in range(2):
            lanes = slice(strand * TRK, (strand + 1) * TRK)
            head_ref[h * DV : h * DV + 128, strand, :] = head[h * 128 : (h + 1) * 128, lanes]
            head_ref[h * DV + 128 : (h + 1) * DV, strand, :] = head[
                512 + h * 64 : 512 + (h + 1) * 64, lanes
            ]


def tail(place, parts, weight, bias, target, strand, sel):
    operands = (*parts, weight, bias, target, strand, sel)
    return pl.pallas_call(
        tail_kernel,
        grid=(1,),
        in_specs=[pl.BlockSpec(memory_space=pltpu.SMEM)]
        + [whole(x.shape) for x in parts]
        + [VMEM] * 5,
        out_specs=(whole((16, 4, TRK)), whole((768, 2, TRK)), whole((2, TRK))),
        out_shape=(
            jax.ShapeDtypeStruct((16, 4, TRK), F32),
            jax.ShapeDtypeStruct((768, 2, TRK), F32),
            jax.ShapeDtypeStruct((2, TRK), F32),
        ),
        scratch_shapes=[
            pltpu.VMEM((512, 768), BF16),
            pltpu.VMEM((512, 768), BF16),
            pltpu.VMEM((768, 768), BF16),
        ],
        compiler_params=pltpu.CompilerParams(vmem_limit_bytes=24 * MIB),
        cost_estimate=pl.CostEstimate(
            flops=4 * 512 * 768 * 768, bytes_accessed=6 * MIB, transcendentals=512 * 384 * 4
        ),
        name="tail",
    )(place, *operands)


def table_kernel(
    place_ref, a_ref, b_ref, key_ref, sel_key_ref, target_ref, strand_ref, sel_ref,
    chosen_ref, table_ref,
):
    for n, ref in enumerate((a_ref, b_ref)):
        for j in range(8):
            at = pl.multiple_of(place_ref[n * 8 + j], 96)
            table_ref[pl.ds(at, 96), :] = ref[j * 96 : (j + 1) * 96, :]
    for group in range(16):
        window = group // 8 * 8 + group % 4 * 2 + group // 4 % 2
        rows = slice(group * 32, (group + 1) * 32)
        info = table_ref[window * 96 + 64 : window * 96 + 96, 0:128].astype(F32)
        key = info[:, 0:1] * 16.0 + float(window)
        chosen_ref[rows, :] = jnp.where(key_ref[...] == key, 1.0, 0.0).astype(BF16)
        sel_ref[rows, :] = jnp.where(sel_key_ref[...] == key, 1.0, 0.0).astype(BF16)
        strand_ref[rows, :] = jnp.broadcast_to(info[:, 1:2], (32, 128))
    target_ref[...] = jnp.dot(
        chosen_ref[...], table_ref[...], preferred_element_type=F32
    ).astype(BF16)


def permute(array, axis, target):
    count = lax.axis_size(axis)
    return lax.ppermute(array, axis, [(i, target(i)) for i in range(count)])


def z_up(s):
    return s // 8 * 8 + (s + 1) % 8


def z_down(s):
    return s // 8 * 8 + (s + 7) % 8


def y_over(s):
    return s ^ 8


def join(x, axis, masks):
    return [permute(x, axis, lambda s, m=m: s ^ m) for m in masks]


def stack_kernel(*refs):
    parts, out_ref = refs[:-1], refs[-1]
    rows = parts[0].shape[0]
    for n, ref in enumerate(parts):
        out_ref[n * rows : (n + 1) * rows, :] = ref[...]


def stacked(parts):
    rows, lanes = parts[0].shape
    return pl.pallas_call(
        stack_kernel,
        in_specs=[VMEM] * len(parts),
        out_specs=VMEM,
        out_shape=jax.ShapeDtypeStruct((len(parts) * rows, lanes), BF16),
        compiler_params=pltpu.CompilerParams(vmem_limit_bytes=4 * MIB),
        name="stacked",
    )(*parts)


def across(x):
    return stacked([x, *join(x, "batch", (8,))])


def spread(both):
    near = stacked([both, *join(both, "batch", (2, 4, 6))])
    return near, *join(near, "batch", (1,))


def gene_tables(gene_target, gene_owner, gene_strand):
    genes = gene_strand.shape[1]
    owner, strand = gene_owner[0, :, 0], gene_strand[0]
    gene = jnp.arange(genes, dtype=jnp.int32)
    earlier = (owner[:, None] == owner[None, :]) & (gene[None, :] < gene[:, None])
    rank = jnp.sum(earlier.astype(jnp.int32), axis=1)
    lane = jnp.arange(TRK, dtype=jnp.int32)[None]
    slot = (owner * 4 + rank)[:, None]
    info = jnp.where(lane == 0, slot, jnp.where(lane == 1, strand[:, None], 0)).astype(BF16)
    mine = jnp.concatenate([gene_target[0].reshape(64, TRK).astype(BF16), info], axis=0)
    return mine


def gene_rows(place, parts):
    row = jnp.arange(16 * 96, dtype=jnp.int32)
    at = row % 96
    key = jnp.where(at < 64, (row // 96 * 4 + at % 4) * 16 + at // 4, -1)
    lane = jnp.arange(128, dtype=jnp.int32)
    sel_key = jnp.where(lane < 64, (lax.axis_index("batch") * 4 + lane % 4) * 16 + lane // 4, -1)
    operands = (*parts, key.astype(F32)[None], sel_key.astype(F32)[None])
    return pl.pallas_call(
        table_kernel,
        grid=(1,),
        in_specs=[pl.BlockSpec(memory_space=pltpu.SMEM)] + [whole(x.shape) for x in operands],
        out_specs=(whole((512, TRK)), whole((512, 128)), whole((512, 128))),
        out_shape=(
            jax.ShapeDtypeStruct((512, TRK), BF16),
            jax.ShapeDtypeStruct((512, 128), F32),
            jax.ShapeDtypeStruct((512, 128), BF16),
        ),
        scratch_shapes=[pltpu.VMEM((512, 16 * 96), BF16), pltpu.VMEM((16 * 96, TRK), BF16)],
        compiler_params=pltpu.CompilerParams(vmem_limit_bytes=16 * MIB),
        cost_estimate=pl.CostEstimate(
            flops=2 * 512 * 1536 * 384, bytes_accessed=3 * MIB, transcendentals=0
        ),
        name="tables",
    )(place, *operands)


def local(
    tokens,
    filter_tap_weight,
    norm_gain,
    query_weight,
    keyval_weight,
    head_weight,
    head_bias,
    exon_start,
    exon_end,
    gene_strand,
    gene_owner,
    gene_target,
):
    rows = tokens[0]
    row_count = rows.shape[0]
    reach = TAPS // 2 * STRIDE
    tie = lax.optimization_barrier
    low = lax.ppermute(rows[row_count - reach :], "seq", [(i, i + 1) for i in range(15)])
    high = lax.ppermute(rows[:reach], "seq", [(i + 1, i) for i in range(15)])

    acc, own, tables = front(
        rows, low, high, filter_tap_weight, norm_gain[None], query_weight, keyval_weight.T,
        gene_tables(gene_target, gene_owner, gene_strand),
    )
    me = lax.axis_index("batch")
    y, x, core = me // 8, me // 2 % 4, me % 2
    near = [x, x ^ 1, x ^ 2, x ^ 3]
    spots = [(b, a, c) for c in (core, 1 - core) for a in near for b in (y, 1 - y)]
    owner_place = jnp.stack([(b * 8 + a * 2 + c) * 96 for b, a, c in spots]).astype(jnp.int32)
    place = jnp.stack([((b * 2 + c) * 4 + a) * 32 for b, a, c in spots]).astype(jnp.int32)
    positions = lax.axis_index("seq") * row_count + jnp.arange(row_count, dtype=jnp.int32)
    starts, stops = exon_start[0], exon_end[0]
    inside = (positions >= starts[:, :, None]) & (positions < stops[:, :, None])
    counts = jnp.sum(inside.astype(F32), axis=1).astype(BF16)
    inv_len = 1.0 / jnp.sum((stops - starts).astype(F32), axis=1, keepdims=True)
    bias = head_bias.reshape(1, 2 * TRK)

    def up(x):
        return permute(x, "seq", z_up)

    def down(x):
        return permute(x, "seq", z_down)

    up1, down1 = up(own), down(own)
    over0 = permute(own, "seq", y_over)
    acc = attend_first(acc, own)
    acc, up1, down1 = tie((acc, up1, down1))
    up2, down2 = up(up1), down(down1)
    over_up1, over_down1 = up(over0), down(over0)
    acc = attend_more(acc, [up1, down1])
    acc, up2, down2 = tie((acc, up2, down2))
    up3, down3 = up(up2), down(down2)
    acc = attend_more(acc, [over0, up2, down2])
    acc, over_up1, over_down1 = tie((acc, over_up1, over_down1))
    over_up2, over_down2 = up(over_up1), down(over_down1)
    acc = attend_more(acc, [over_up1, over_down1])
    acc, up3, down3, tables, head_weight = tie((acc, up3, down3, tables, head_weight))
    tables = spread(tables)
    up4 = up(up3)
    acc = attend_more(acc, [up3, down3])
    acc, over_up2, over_down2 = tie((acc, over_up2, over_down2))
    over_up3, over_down3 = up(over_up2), down(over_down2)
    acc = attend_more(acc, [over_up2, over_down2])
    target, strand, sel = gene_rows(owner_place, tables)
    acc, over_down3, target, strand, sel = tie((acc, over_down3, target, strand, sel))
    over_down4 = down(over_down3)
    acc = attend_more(acc, [up4, over_down3])
    att, pool = attend_last(acc, counts, inv_len, [over_up3, over_down4])

    weight = head_weight.reshape(HEADS * DV, 2 * TRK)
    coverage = coverage_of(att, weight, bias).reshape(1, row_count, 2, TRK)
    for masks in ((1, 8, 9), (2, 4, 6)):
        pieces, coverage = tie((join(pool, "seq", masks), coverage))
        a, b, c = [piece.astype(F32) for piece in pieces]
        pool = ((pool.astype(F32) + a) + (b + c)).astype(BF16)
    pred, head_grad, bias_grad = tail(
        place, spread(across(pool)), weight, bias, target, strand, sel
    )
    return (
        coverage,
        pred[None],
        head_grad,
        bias_grad,
    )


def solution(mesh):
    in_specs = (
        P("batch", "seq", None),
        P(),
        P(),
        P(),
        P(),
        P(),
        P(),
        P("batch", None, None),
        P("batch", None, None),
        P("batch", None),
        P("batch", None, None),
        P("batch", None, None, None),
    )
    out_specs = (P("batch", "seq", None, None), P("batch", None, None, None), P(), P())
    return jax.shard_map(local, mesh=mesh, in_specs=in_specs, out_specs=out_specs, check_vma=False)
```
